256 devices in a mesh: date: 8 (over x, y_hi), path: 32 (over z, y_lo, core).
Axes of the slice: x: 4, y: 4 (y_hi: 2, y_lo: 2; y = y_hi * 2 + y_lo), z: 8, core: 2. Of those that a mesh axis runs over, the one named last changes fastest.
Arguments:
- factors: bfloat16 [64, 16, 131072], P('date', None, 'path'), may hold values from -10 to 10
- cashflows: bfloat16 [64, 64, 131072], P('date', None, 'path'), may hold values from -12 to 12
- frequency: bfloat16 [128, 16], replicated, may hold values from -1.5 to 1.5
- phases: float32 [128], replicated, may hold values from -3.140625 to 3.140625
- margin_lag: int32 [64], replicated, may hold values from 1 to 2
- thresholds: int32 [64], replicated, may hold values from 0 to 149
- transfer_min: int32 [64], replicated, may hold values from 0 to 59
Outputs:
- exposure: bfloat16 [64, 64, 131072], P('date', None, 'path')
- profile: float32 [64, 64], P('date')
The draws below stay inside these ranges and needn't reach their ends.
All inputs are finite; a program needn't handle non-finite values.
Results may differ from the reference program's by a relative error of at most 0.0058.
Values may be sent and summed in bfloat16 or wider, within the bound.
No kernel may reach another device: no remote copies, remote signals or barrier semaphores. Data moves between devices by JAX's collectives and lax.ppermute only.
A program may use at most 128 MiB of HBM per device.

```python
import jax
import jax.numpy as jnp
from jax import lax

K = 128
NS = 64
R = 16
LAG_MAX = 2
DATES = 64
PATHS = 131072


def make_factors(key):
    scaled = jnp.clip(jax.random.normal(jax.random.fold_in(key, 11), (DATES, R, PATHS), jnp.float32), -5.0, 5.0)
    return scaled


def draw_factors(key, part):
    return make_factors(key).astype(jnp.bfloat16)


def draw_cashflows(key, part):
    scaled = make_factors(key)
    mixing = jax.random.normal(jax.random.fold_in(key, 13), (DATES, NS, R), jnp.float32) * (1.5 / R ** 0.5)
    signal = jnp.einsum('tnr,trp->tnp', mixing, scaled)
    noise_part = 0.4 * jax.random.normal(jax.random.fold_in(key, 14), (DATES, NS, PATHS), jnp.float32)
    flows = jnp.tanh(signal) + 0.3 * signal + noise_part
    return jnp.clip(flows, -12.0, 12.0).astype(jnp.bfloat16)


def touch_ends(drawn, key, least, top_value):
    shape = drawn.shape
    place = [jax.random.randint(jax.random.fold_in(key, axis), (), 0, shape[axis]) for axis in range(len(shape))]
    drawn = drawn.at[tuple(place)].set(least)
    longest = shape.index(max(shape))
    place[longest] = (place[longest] + 1) % shape[longest]
    return drawn.at[tuple(place)].set(top_value)


def bell_draw(stream_key, dims, scale, bound, held_as=jnp.bfloat16):
    drawn = scale * jax.random.normal(stream_key, dims, jnp.float32)
    return jnp.clip(drawn, min=-bound, max=bound).astype(held_as)


def setup_inputs(seed: int = 0) -> dict:
    streams_of = jax.random.split(jax.random.key(seed), 8)
    return {
        "factors": draw_factors(jax.random.fold_in(streams_of[7], 71), 0),
        "cashflows": draw_cashflows(jax.random.fold_in(streams_of[7], 71), 0),
        "frequency": bell_draw(streams_of[2], (K, R), R ** -0.5, 1.5),
        "phases": jnp.clip(jax.random.uniform(streams_of[3], (K,), jnp.float32, -3.140625, 3.140625), -3.140625, 3.140625),
        "margin_lag": touch_ends(jax.random.randint(streams_of[4], (NS,), 1, LAG_MAX + 1), jax.random.fold_in(streams_of[4], 1), 1, LAG_MAX).astype(jnp.int32),
        "thresholds": touch_ends(jax.random.randint(streams_of[5], (NS,), 0, 150), jax.random.fold_in(streams_of[5], 1), 0, 149).astype(jnp.int32),
        "transfer_min": touch_ends(jax.random.randint(streams_of[6], (NS,), 0, 60), jax.random.fold_in(streams_of[6], 1), 0, 59).astype(jnp.int32),
    }


ridge_weight = 0.05
root_two = 1.4142135623730951

def regress(gram_sum, right_sum, paths_all):
    system = gram_sum / paths_all + ridge_weight * jnp.eye(gram_sum.shape[-1], dtype=jnp.float32)
    factor = lax.linalg.cholesky(system)
    solved = lax.linalg.triangular_solve(factor, right_sum / paths_all, left_side=True, lower=True)
    solved = lax.linalg.triangular_solve(factor, solved, left_side=True, lower=True, transpose_a=True)
    return solved.astype(jnp.bfloat16)

def reference(factors, cashflows, frequency, phases, margin_lag, thresholds, transfer_min):
    paths_all = factors.shape[2]

    def one_date(inputs):
        state_now, flows_now = inputs
        angles = jnp.dot(frequency.astype(jnp.float32), state_now.astype(jnp.float32)) + phases[:, None]
        features = (root_two * jnp.cos(angles)).astype(jnp.bfloat16)
        gram_sum = jnp.dot(features.astype(jnp.float32), features.T.astype(jnp.float32), preferred_element_type=jnp.float32)
        right_sum = jnp.dot(features.astype(jnp.float32), flows_now.T.astype(jnp.float32), preferred_element_type=jnp.float32)
        coefficients = regress(gram_sum, right_sum, paths_all)
        return jnp.dot(coefficients.T.astype(jnp.float32), features.astype(jnp.float32), preferred_element_type=jnp.float32).astype(jnp.bfloat16)
    values = lax.map(one_date, (factors, cashflows))
    offset = (thresholds + transfer_min).astype(jnp.float32) / 100.0

    def expose(date_index):
        current = lax.dynamic_index_in_dim(values, date_index, 0, keepdims=False).astype(jnp.float32)
        lagged = jnp.zeros_like(current)
        for lag_value in range(1, LAG_MAX + 1):
            source = date_index - lag_value
            shifted = lax.dynamic_index_in_dim(values, jnp.maximum(source, 0).astype(jnp.int32), 0, keepdims=False).astype(jnp.float32)
            shifted = jnp.where(source >= 0, shifted, jnp.zeros_like(shifted))
            lagged = jnp.where((margin_lag == lag_value)[:, None], shifted, lagged)
        collateral = jnp.maximum(lagged - offset[:, None], 0.0)
        exposure = jnp.maximum(current - collateral, 0.0)
        return (exposure.astype(jnp.bfloat16), jnp.sum(exposure, axis=1) / paths_all)
    exposure, profile = lax.map(expose, jnp.arange(values.shape[0], dtype=jnp.int32))
    return (exposure, profile)
```

```python
import functools

import jax
import jax.numpy as jnp
from jax import lax
from jax.experimental import pallas as pl
from jax.experimental.pallas import tpu as pltpu
from jax.sharding import PartitionSpec as P

LAG_MAX = 2
ridge_weight = 0.05
COS_TERMS = (
    1.4142124652862549,
    -27.915136337280273,
    91.82308197021484,
    -120.5933837890625,
    83.14732360839844,
    -29.807071685791016,
)
ROUNDER = 12582912.0
INV_TWO_PI = 0.15915494309189535
CHUNK = 512


def three_parts(x):
    hi = x.astype(jnp.bfloat16)
    rest = x - hi.astype(jnp.float32)
    mid = rest.astype(jnp.bfloat16)
    low = (rest - mid.astype(jnp.float32)).astype(jnp.bfloat16)
    return hi, mid, low


def turn_weights(freq_ref, phase_ref):
    k, r = freq_ref.shape
    parts = three_parts(freq_ref[...].astype(jnp.float32) * INV_TWO_PI)
    column = jnp.broadcast_to(phase_ref[...] * INV_TWO_PI, (k, k)).T[:, :r]
    place = lax.broadcasted_iota(jnp.int32, (k, r), 1)
    tail = jnp.zeros((k, r), jnp.float32)
    for i, part in enumerate(three_parts(column)):
        tail = jnp.where(place == i, part.astype(jnp.float32), tail)
    return jnp.concatenate([*parts, tail.astype(jnp.bfloat16)], axis=1)


def chunk_features(weights, x):
    ones = jnp.ones(x.shape, jnp.bfloat16)
    turns = jnp.dot(
        weights, jnp.concatenate([x, x, x, ones], axis=0), preferred_element_type=jnp.float32
    )
    part = turns - ((turns + ROUNDER) - ROUNDER)
    s = part * part
    total = jnp.full(s.shape, COS_TERMS[-1], jnp.float32)
    for term in COS_TERMS[-2::-1]:
        total = total * s + term
    return total.astype(jnp.bfloat16)


def features_kernel(freq_ref, phase_ref, factors_ref, features_ref, weights_ref):
    @pl.when(pl.program_id(0) == 0)
    def _():
        weights_ref[...] = turn_weights(freq_ref, phase_ref)

    for at in range(0, factors_ref.shape[2], CHUNK):
        span = pl.ds(at, CHUNK)
        features_ref[0, :, span] = chunk_features(weights_ref[...], factors_ref[0, :, span])


def sums_kernel(freq_ref, phase_ref, factors_ref, flows_ref, features_ref, sums_ref, weights_ref):
    @pl.when(pl.program_id(0) == 0)
    def _():
        weights_ref[...] = turn_weights(freq_ref, phase_ref)

    k = freq_ref.shape[0]
    dims = (((1,), (1,)), ((), ()))
    gram = jnp.zeros((k, k), jnp.float32)
    right = jnp.zeros((flows_ref.shape[1], k), jnp.float32)
    for at in range(0, factors_ref.shape[2], CHUNK):
        span = pl.ds(at, CHUNK)
        feats = chunk_features(weights_ref[...], factors_ref[0, :, span])
        features_ref[0, :, span] = feats
        gram += lax.dot_general(feats, feats, dims, preferred_element_type=jnp.float32)
        right += lax.dot_general(
            flows_ref[0, :, span], feats, dims, preferred_element_type=jnp.float32
        )
    sums_ref[0, :k, :] = gram
    sums_ref[0, k:, :] = right


def whole(a):
    return pl.BlockSpec(a.shape, lambda t: (0,) * a.ndim)


def per_date(a):
    return pl.BlockSpec((1, *a.shape[1:]), lambda t: (t,) + (0,) * (a.ndim - 1))


def params(limit=48 << 20):
    return pltpu.CompilerParams(vmem_limit_bytes=limit)


def features_of(frequency, phases, factors):
    dates, r, paths = factors.shape
    k = frequency.shape[0]
    out = jax.ShapeDtypeStruct((dates, k, paths), jnp.bfloat16)
    return pl.pallas_call(
        features_kernel,
        grid=(dates,),
        in_specs=[whole(frequency), whole(phases), per_date(factors)],
        out_specs=per_date(out),
        out_shape=out,
        scratch_shapes=[pltpu.VMEM((k, 4 * r), jnp.bfloat16)],
        compiler_params=params(),
        cost_estimate=pl.CostEstimate(
            flops=16 * dates * k * paths, bytes_accessed=2 * dates * k * paths, transcendentals=0
        ),
        name="features",
    )(frequency, phases, factors)


def sums_of(frequency, phases, factors, flows):
    dates, r, paths = factors.shape
    k, sets = frequency.shape[0], flows.shape[1]
    outs = (
        jax.ShapeDtypeStruct((dates, k, paths), jnp.bfloat16),
        jax.ShapeDtypeStruct((dates, k + sets, k), jnp.float32),
    )
    return pl.pallas_call(
        sums_kernel,
        grid=(dates,),
        in_specs=[whole(frequency), whole(phases), per_date(factors), per_date(flows)],
        out_specs=tuple(per_date(o) for o in outs),
        out_shape=outs,
        scratch_shapes=[pltpu.VMEM((k, 4 * r), jnp.bfloat16)],
        compiler_params=params(),
        cost_estimate=pl.CostEstimate(
            flops=400 * dates * k * paths, bytes_accessed=4 * dates * k * paths, transcendentals=0
        ),
        name="sums",
    )(frequency, phases, factors, flows)


def solve_kernel(paths_all, one_ref, two_ref, out_ref):
    k = one_ref.shape[1]
    total = (one_ref[...] + two_ref[...]) / paths_all
    row_at = lax.broadcasted_iota(jnp.int32, (k, k), 0)
    lane_at = lax.broadcasted_iota(jnp.int32, (k, k), 1)
    system = total[:k] + jnp.where(row_at == lane_at, ridge_weight, 0.0)
    m = jnp.concatenate([system, total[k:]], axis=0)
    lane = lax.broadcasted_iota(jnp.int32, (1, k), 1)
    for j in range(k):
        top = j // 8 * 8
        row = m[j - (k + 64 - m.shape[0]) : j - (k + 64 - m.shape[0]) + 1, :]
        pivot = 1.0 / row[:, j : j + 1]
        scaled = jnp.where(lane == j, 1.0 - pivot, row * pivot)
        if (j + 1) % 8 == 0:
            m = m[8:, :]
        m = m - m[:, j : j + 1] * scaled
    out_ref[...] = m.astype(jnp.bfloat16)


def solved(one, two, paths_all):
    k = one.shape[1]
    sets = one.shape[0] - k
    return pl.pallas_call(
        functools.partial(solve_kernel, paths_all),
        out_shape=jax.ShapeDtypeStruct((sets, k), jnp.bfloat16),
        compiler_params=params(),
        name="solve",
    )(one, two)


def exposure_kernel(
    paths_all,
    lag_ref,
    threshold_ref,
    transfer_ref,
    coefs_ref,
    prior_coefs_ref,
    features_ref,
    prior_features_ref,
    exposure_ref,
    profile_ref,
    old_ref,
    sums_ref,
):
    t = pl.program_id(0)
    dates = pl.num_programs(0)
    sets, paths = exposure_ref.shape[1:]
    slots = LAG_MAX + 1

    def value(coefs, feats):
        return jnp.dot(coefs, feats, preferred_element_type=jnp.float32).astype(jnp.bfloat16)

    @pl.when(t == 0)
    def _():
        for i in range(LAG_MAX):
            for at in range(0, paths, CHUNK):
                span = pl.ds(at, CHUNK)
                old_ref[i + 1, :, span] = value(prior_coefs_ref[i], prior_features_ref[i, :, span])

    def column(ref):
        return jnp.broadcast_to(ref[...], (128, sets)).T

    offset = (column(threshold_ref) + column(transfer_ref)).astype(jnp.float32) / 100.0
    recent = column(lag_ref) == 1
    wide = (sets, CHUNK)
    offset = jnp.concatenate([offset] * (CHUNK // 128), axis=1)
    recent = jnp.concatenate([recent.astype(jnp.float32)] * (CHUNK // 128), axis=1) > 0.5
    total = jnp.zeros((sets, 128), jnp.float32)
    now = lax.rem(t, slots)
    last = lax.rem(t + LAG_MAX, slots)
    before = lax.rem(t + 1, slots)
    for at in range(0, paths, CHUNK):
        span = pl.ds(at, CHUNK)
        v = value(coefs_ref[0], features_ref[0, :, span])
        lagged = jnp.where(
            recent,
            old_ref[last, :, span].astype(jnp.float32),
            old_ref[before, :, span].astype(jnp.float32),
        )
        old_ref[now, :, span] = v
        collateral = jnp.maximum(lagged - offset, 0.0)
        exposed = jnp.maximum(v.astype(jnp.float32) - collateral, 0.0)
        exposure_ref[0, :, span] = exposed.astype(jnp.bfloat16)
        for i in range(0, CHUNK, 128):
            total += exposed[:, i : i + 128]
    here = jnp.sum(total, axis=1, keepdims=True) / paths_all
    lane = lax.broadcasted_iota(jnp.int32, (sets, 128), 1)

    @pl.when(t == 0)
    def _():
        sums_ref[...] = jnp.zeros(sums_ref.shape, jnp.float32)

    sums_ref[...] = jnp.where(lane == t, here, sums_ref[...])

    @pl.when(t == dates - 1)
    def _():
        profile_ref[...] = sums_ref[...].T[: profile_ref.shape[0]]


def exposures(lag, threshold, transfer, coefs, prior_coefs, features, prior_features, paths_all):
    dates, k, paths = features.shape
    sets = coefs.shape[1]
    outs = (
        jax.ShapeDtypeStruct((dates, sets, paths), jnp.bfloat16),
        jax.ShapeDtypeStruct((dates, sets), jnp.float32),
    )
    args = (lag, threshold, transfer, coefs, prior_coefs, features, prior_features)
    return pl.pallas_call(
        functools.partial(exposure_kernel, paths_all),
        grid=(dates,),
        in_specs=[
            whole(lag),
            whole(threshold),
            whole(transfer),
            per_date(coefs),
            whole(prior_coefs),
            per_date(features),
            whole(prior_features),
        ],
        out_specs=(per_date(outs[0]), whole(outs[1])),
        out_shape=outs,
        scratch_shapes=[
            pltpu.VMEM((LAG_MAX + 1, sets, paths), jnp.bfloat16),
            pltpu.VMEM((sets, 128), jnp.float32),
        ],
        compiler_params=params(),
        cost_estimate=pl.CostEstimate(
            flops=2 * dates * k * sets * paths,
            bytes_accessed=2 * dates * (k + sets) * paths,
            transcendentals=0,
        ),
        name="exposure",
    )(*args)


def by_core(i):
    return i ^ 1


def by_row(i):
    return i ^ 2


def by_near(i):
    return i ^ 4


def by_next(i):
    return i ^ 8


def by_far(i):
    z = i // 4
    return (6 - z + 2 * (z % 2)) % 8 * 4 + i % 4


def swapped(value, partner):
    length = lax.axis_size("path")
    return lax.ppermute(value, "path", [(i, partner(i)) for i in range(length)])


def halved(value, partner, bit):
    other = lax.dynamic_index_in_dim(value, 1 - bit, 0, keepdims=False)
    mine = lax.dynamic_index_in_dim(value, bit, 0, keepdims=False)
    return mine + swapped(other, partner)


def doubled(value, partner, bit):
    other = swapped(value, partner)
    low = jnp.where(bit == 0, value, other)
    high = jnp.where(bit == 0, other, value)
    return jnp.concatenate([low, high], axis=0)


def from_earlier(value):
    length = lax.axis_size("date")
    return lax.ppermute(value, "date", [(i, i + 1) for i in range(length - 1)])


def local(factors, cashflows, frequency, phases, margin_lag, thresholds, transfer_min):
    paths_all = factors.shape[2] * lax.axis_size("path")
    me = lax.axis_index("path")
    core, row, near = me % 2, me // 2 % 2, me // 4 % 2
    prior_factors = from_earlier(factors[-LAG_MAX:])
    phases = phases.reshape(1, -1)
    features, sums = sums_of(frequency, phases, factors, cashflows)
    kept = halved(sums.reshape(2, 4, *sums.shape[1:]), by_core, core)
    kept = halved(kept.reshape(2, 2, *sums.shape[1:]), by_row, row)
    kept = halved(kept, by_near, near)
    kept = kept + swapped(kept, by_next)
    coefs = solved(kept, swapped(kept, by_far), paths_all)
    prior_features = features_of(frequency, phases, prior_factors)
    coefs = doubled(coefs[None], by_near, near)
    coefs = doubled(coefs, by_row, row)
    coefs = doubled(coefs, by_core, core)
    prior_coefs = from_earlier(coefs[-LAG_MAX:])
    exposure, profile = exposures(
        margin_lag.reshape(1, -1),
        thresholds.reshape(1, -1),
        transfer_min.reshape(1, -1),
        coefs,
        prior_coefs,
        features,
        prior_features,
        paths_all,
    )
    for partner in (by_core, by_row, by_near, by_next, by_far):
        profile = profile + swapped(profile, partner)
    return exposure, profile


def solution(mesh):
    return jax.shard_map(
        local,
        mesh=mesh,
        in_specs=(P("date", None, "path"), P("date", None, "path"), P(), P(), P(), P(), P()),
        out_specs=(P("date", None, "path"), P("date", None)),
        check_vma=False,
    )
```

```python
import functools

import jax
import jax.numpy as jnp
from jax import lax
from jax.experimental import pallas as pl
from jax.experimental.pallas import tpu as pltpu
from jax.sharding import PartitionSpec as P

LAG_MAX = 2
ridge_weight = 0.05
COS_TERMS = (
    1.4142124652862549,
    -27.915136337280273,
    91.82308197021484,
    -120.5933837890625,
    83.14732360839844,
    -29.807071685791016,
)
ROUNDER = 12582912.0
INV_TWO_PI = 0.15915494309189535
CHUNK = 512


def three_parts(x):
    hi = x.astype(jnp.bfloat16)
    rest = x - hi.astype(jnp.float32)
    mid = rest.astype(jnp.bfloat16)
    low = (rest - mid.astype(jnp.float32)).astype(jnp.bfloat16)
    return hi, mid, low


def turn_weights(freq_ref, phase_ref):
    r, k = freq_ref.shape
    rows = three_parts(freq_ref[...].astype(jnp.float32) * INV_TWO_PI)
    phase = three_parts(phase_ref[...] * INV_TWO_PI)
    rows = [part.astype(jnp.float32) for part in rows + phase]
    rest = jnp.zeros((r - len(phase), k), jnp.float32)
    return jnp.concatenate([*rows, rest], axis=0).T.astype(jnp.bfloat16)


def chunk_turns(weights, x):
    ones = jnp.ones(x.shape, jnp.bfloat16)
    return jnp.dot(
        weights, jnp.concatenate([x, x, x, ones], axis=0), preferred_element_type=jnp.float32
    )


def cosines(turns):
    part = turns - ((turns + ROUNDER) - ROUNDER)
    s = part * part
    total = jnp.full(s.shape, COS_TERMS[-1], jnp.float32)
    for term in COS_TERMS[-2::-1]:
        total = total * s + term
    return total.astype(jnp.bfloat16)


def features_kernel(freq_ref, phase_ref, factors_ref, features_ref, weights_ref):
    @pl.when(pl.program_id(0) == 0)
    def _():
        weights_ref[...] = turn_weights(freq_ref, phase_ref)

    for at in range(0, factors_ref.shape[2], CHUNK):
        span = pl.ds(at, CHUNK)
        features_ref[0, :, span] = cosines(chunk_turns(weights_ref[...], factors_ref[0, :, span]))


def sums_kernel(freq_ref, phase_ref, factors_ref, flows_ref, features_ref, sums_ref, weights_ref):
    @pl.when(pl.program_id(0) == 0)
    def _():
        weights_ref[...] = turn_weights(freq_ref, phase_ref)

    spans = [pl.ds(at, CHUNK) for at in range(0, factors_ref.shape[2], CHUNK)]
    weights = weights_ref[...]

    def turns_of(i):
        return chunk_turns(weights, factors_ref[0, :, spans[i]])

    def add_products(sums, i, feats):
        both = jnp.concatenate([feats, flows_ref[0, :, spans[i]]], axis=0)
        product = lax.dot_general(
            both, feats, (((1,), (1,)), ((), ())), preferred_element_type=jnp.float32
        )
        return product if sums is None else sums + product

    sums, before = None, None
    turns = turns_of(0)
    for i, span in enumerate(spans):
        later = turns_of(i + 1) if i + 1 < len(spans) else None
        if i:
            sums = add_products(sums, i - 1, before)
        before = cosines(turns)
        features_ref[0, :, span] = before
        turns = later
    sums_ref[0] = add_products(sums, len(spans) - 1, before)


def whole(a):
    return pl.BlockSpec(a.shape, lambda t: (0,) * a.ndim)


def per_date(a):
    return pl.BlockSpec((1, *a.shape[1:]), lambda t: (t,) + (0,) * (a.ndim - 1))


def in_hbm(a):
    return pltpu.with_memory_space_constraint(a, pltpu.HBM)


def params(limit=48 << 20):
    return pltpu.CompilerParams(vmem_limit_bytes=limit)


def features_of(frequency, phases, factors):
    dates, r, paths = factors.shape
    k = frequency.shape[1]
    out = jax.ShapeDtypeStruct((dates, k, paths), jnp.bfloat16)
    return pl.pallas_call(
        features_kernel,
        grid=(dates,),
        in_specs=[whole(frequency), whole(phases), per_date(factors)],
        out_specs=per_date(out),
        out_shape=out,
        scratch_shapes=[pltpu.VMEM((k, 4 * r), jnp.bfloat16)],
        compiler_params=params(),
        cost_estimate=pl.CostEstimate(
            flops=16 * dates * k * paths, bytes_accessed=2 * dates * k * paths, transcendentals=0
        ),
        name="features",
    )(frequency, phases, factors)


def sums_of(frequency, phases, factors, flows):
    dates, r, paths = factors.shape
    k, sets = frequency.shape[1], flows.shape[1]
    outs = (
        jax.ShapeDtypeStruct((dates, k, paths), jnp.bfloat16),
        jax.ShapeDtypeStruct((dates, k + sets, k), jnp.float32),
    )
    return pl.pallas_call(
        sums_kernel,
        grid=(dates,),
        in_specs=[whole(frequency), whole(phases), per_date(factors), per_date(flows)],
        out_specs=tuple(per_date(o) for o in outs),
        out_shape=outs,
        scratch_shapes=[pltpu.VMEM((k, 4 * r), jnp.bfloat16)],
        compiler_params=params(),
        cost_estimate=pl.CostEstimate(
            flops=400 * dates * k * paths, bytes_accessed=4 * dates * k * paths, transcendentals=0
        ),
        name="sums",
    )(frequency, phases, factors, flows)


def solve_kernel(paths_all, one_ref, two_ref, out_ref):
    k = one_ref.shape[1]
    total = (one_ref[...] + two_ref[...]) / paths_all
    row_at = lax.broadcasted_iota(jnp.int32, (k, k), 0)
    lane_at = lax.broadcasted_iota(jnp.int32, (k, k), 1)
    system = total[:k] + jnp.where(row_at == lane_at, ridge_weight, 0.0)
    m = jnp.concatenate([system, total[k:]], axis=0)
    lane = lax.broadcasted_iota(jnp.int32, (1, k), 1)
    for j in range(k):
        top = j // 8 * 8
        row = m[j - (k + 64 - m.shape[0]) : j - (k + 64 - m.shape[0]) + 1, :]
        pivot = 1.0 / row[:, j : j + 1]
        scaled = jnp.where(lane == j, 1.0 - pivot, row * pivot)
        if (j + 1) % 8 == 0:
            m = m[8:, :]
        m = m - m[:, j : j + 1] * scaled
    out_ref[...] = m.astype(jnp.bfloat16)


def solved(one, two, paths_all):
    k = one.shape[1]
    sets = one.shape[0] - k
    return pl.pallas_call(
        functools.partial(solve_kernel, paths_all),
        out_shape=jax.ShapeDtypeStruct((sets, k), jnp.bfloat16),
        compiler_params=params(),
        name="solve",
    )(one, two)


def value_of(coefs, feats):
    return jnp.dot(coefs, feats, preferred_element_type=jnp.float32).astype(jnp.bfloat16)


def limits_of(lag_ref, threshold_ref, transfer_ref):
    def column(ref):
        return jnp.broadcast_to(ref[...], (128, ref.shape[1])).T

    offset = (column(threshold_ref) + column(transfer_ref)).astype(jnp.float32) / 100.0
    recent = jnp.where(column(lag_ref) == 1, 1.0, 0.0)
    times = CHUNK // 128
    return jnp.concatenate([offset] * times, axis=1), jnp.concatenate([recent] * times, axis=1) > 0.5


def exposed_of(v, last, before, offset, recent):
    lagged = jnp.where(recent, last.astype(jnp.float32), before.astype(jnp.float32))
    collateral = jnp.maximum(lagged - offset, 0.0)
    return jnp.maximum(v.astype(jnp.float32) - collateral, 0.0)


def by_lane(exposed):
    return sum(exposed[:, i : i + 128] for i in range(0, exposed.shape[1], 128))


def later_kernel(
    paths_all,
    lag_ref,
    threshold_ref,
    transfer_ref,
    coefs_ref,
    features_ref,
    exposure_ref,
    profile_ref,
    old_ref,
    sums_ref,
):
    t = pl.program_id(0)
    sets, paths = exposure_ref.shape[1:]
    slots = LAG_MAX + 1
    now, last, before = lax.rem(t, slots), lax.rem(t + LAG_MAX, slots), lax.rem(t + 1, slots)

    @pl.when(t == 0)
    def _():
        sums_ref[...] = jnp.zeros(sums_ref.shape, jnp.float32)

    @pl.when(t < LAG_MAX)
    def _():
        for at in range(0, paths, CHUNK):
            span = pl.ds(at, CHUNK)
            old_ref[now, :, span] = value_of(coefs_ref[0], features_ref[0, :, span])

    @pl.when(t >= LAG_MAX)
    def _():
        offset, recent = limits_of(lag_ref, threshold_ref, transfer_ref)
        total = jnp.zeros((sets, 128), jnp.float32)
        for at in range(0, paths, CHUNK):
            span = pl.ds(at, CHUNK)
            v = value_of(coefs_ref[0], features_ref[0, :, span])
            exposed = exposed_of(v, old_ref[last, :, span], old_ref[before, :, span], offset, recent)
            old_ref[now, :, span] = v
            exposure_ref[0, :, span] = exposed.astype(jnp.bfloat16)
            total += by_lane(exposed)
        here = jnp.sum(total, axis=1, keepdims=True) / paths_all
        lane = lax.broadcasted_iota(jnp.int32, (sets, 128), 1)
        sums_ref[...] = jnp.where(lane == t, here, sums_ref[...])

    @pl.when(t == pl.num_programs(0) - 1)
    def _():
        profile_ref[...] = sums_ref[...].T[: profile_ref.shape[0]]


def first_kernel(
    paths_all,
    lag_ref,
    threshold_ref,
    transfer_ref,
    coefs_ref,
    prior_coefs_ref,
    features_ref,
    prior_features_ref,
    profile_in_ref,
    exposure_in_ref,
    exposure_ref,
    profile_ref,
):
    del exposure_in_ref
    sets, paths = exposure_ref.shape[1:]
    offset, recent = limits_of(lag_ref, threshold_ref, transfer_ref)
    totals = [jnp.zeros((sets, 128), jnp.float32)] * LAG_MAX
    for at in range(0, paths, CHUNK):
        span = pl.ds(at, CHUNK)
        v = [value_of(prior_coefs_ref[i], prior_features_ref[i, :, span]) for i in range(LAG_MAX)]
        for t in range(LAG_MAX):
            v.append(value_of(coefs_ref[t], features_ref[t, :, span]))
            exposed = exposed_of(v[-1], v[-2], v[-3], offset, recent)
            exposure_ref[t, :, span] = exposed.astype(jnp.bfloat16)
            totals[t] = totals[t] + by_lane(exposed)
    lane = lax.broadcasted_iota(jnp.int32, (sets, 128), 1)
    sums = jnp.zeros((sets, 128), jnp.float32)
    for t, total in enumerate(totals):
        here = jnp.sum(total, axis=1, keepdims=True) / paths_all
        sums = jnp.where(lane == t, here, sums)
    profile_ref[...] = profile_in_ref[...] + sums.T[: profile_ref.shape[0]]


def later_exposures(limits, coefs, features, paths_all):
    dates, k, paths = features.shape
    sets = coefs.shape[1]
    outs = (
        jax.ShapeDtypeStruct((dates, sets, paths), jnp.bfloat16),
        jax.ShapeDtypeStruct((dates, sets), jnp.float32),
    )
    return pl.pallas_call(
        functools.partial(later_kernel, paths_all),
        grid=(dates,),
        in_specs=[*(whole(a) for a in limits), per_date(coefs), per_date(features)],
        out_specs=(
            pl.BlockSpec((1, sets, paths), lambda t: (jnp.maximum(t, LAG_MAX), 0, 0)),
            whole(outs[1]),
        ),
        out_shape=outs,
        scratch_shapes=[
            pltpu.VMEM((LAG_MAX + 1, sets, paths), jnp.bfloat16),
            pltpu.VMEM((sets, 128), jnp.float32),
        ],
        compiler_params=params(),
        cost_estimate=pl.CostEstimate(
            flops=2 * dates * k * sets * paths,
            bytes_accessed=2 * dates * (k + sets) * paths,
            transcendentals=0,
        ),
        name="later",
    )(*limits, coefs, features)


def first_exposures(
    limits, coefs, prior_coefs, features, prior_features, profile, exposure, paths_all
):
    dates, sets, paths = exposure.shape
    args = (*limits, coefs, prior_coefs, features, prior_features, profile, exposure)

    def leading(a):
        return pl.BlockSpec((LAG_MAX, *a.shape[1:]), lambda t: (0,) * a.ndim)

    return pl.pallas_call(
        functools.partial(first_kernel, paths_all),
        grid=(1,),
        in_specs=[
            *(whole(a) for a in limits),
            leading(coefs),
            leading(prior_coefs),
            leading(features),
            leading(prior_features),
            whole(profile),
            pl.BlockSpec(memory_space=pl.ANY),
        ],
        out_specs=(leading(exposure), whole(profile)),
        out_shape=(
            jax.ShapeDtypeStruct(exposure.shape, exposure.dtype),
            jax.ShapeDtypeStruct(profile.shape, profile.dtype),
        ),
        input_output_aliases={len(args) - 1: 0},
        compiler_params=params(),
        name="first",
    )(*args)


CORE, ROW, NEAR, NEXT, FAR = 1, 2, 4, 8, 24


def swapped(value, step):
    length = lax.axis_size("path")
    return lax.ppermute(value, "path", [(i, i ^ step) for i in range(1, length, 2)])


def to_odd(value):
    return lax.ppermute(value, "path", [(i, i + 1) for i in range(0, lax.axis_size("path"), 2)])


def to_even(value):
    return lax.ppermute(value, "path", [(i + 1, i) for i in range(0, lax.axis_size("path"), 2)])


def halved(value, step, bit):
    value = value.reshape(2, value.shape[0] // 2, *value.shape[1:])
    other = lax.dynamic_index_in_dim(value, 1 - bit, 0, keepdims=False)
    mine = lax.dynamic_index_in_dim(value, bit, 0, keepdims=False)
    return mine + swapped(other, step)


def doubled(value, step, bit):
    other = swapped(value, step)
    low = jnp.where(bit == 0, value, other)
    high = jnp.where(bit == 0, other, value)
    return jnp.concatenate([low, high], axis=0)


def from_earlier(value):
    length = lax.axis_size("date")
    return lax.ppermute(value, "date", [(i, i + 1) for i in range(length - 1)])


def local(factors, cashflows, frequency, phases, margin_lag, thresholds, transfer_min):
    paths_all = factors.shape[2] * lax.axis_size("path")
    me = lax.axis_index("path")
    odd, row, near = me & 1, (me >> 1) & 1, (me >> 2) & 1
    following = ((me >> 3) ^ (me >> 4)) & 1
    prior_factors = from_earlier(factors[-LAG_MAX:])
    phases = phases.reshape(1, -1)
    frequency = frequency.T
    features, sums = sums_of(frequency, phases, in_hbm(factors), in_hbm(cashflows))
    kept = sums + to_odd(sums)
    kept = halved(kept, ROW, row)
    prior_features = features_of(frequency, phases, prior_factors)
    kept, prior_features = lax.optimization_barrier((kept, prior_features))
    kept = halved(kept, NEAR, near)
    kept = halved(kept, NEXT, following)[0]
    coefs = solved(kept, swapped(kept, FAR), paths_all)
    coefs = doubled(coefs[None], NEXT, following)
    coefs = doubled(coefs, NEAR, near)
    coefs = doubled(coefs, ROW, row)
    coefs = jnp.where(odd == 1, coefs, to_even(coefs))
    prior_coefs = from_earlier(coefs[-LAG_MAX:])
    limits = tuple(a.reshape(1, -1) for a in (margin_lag, thresholds, transfer_min))
    exposure, profile = later_exposures(limits, coefs, features, paths_all)
    exposure, profile = first_exposures(
        limits, coefs, prior_coefs, features, prior_features, profile, exposure, paths_all
    )
    profile = profile + to_odd(profile)
    for step in (ROW, NEAR, NEXT, FAR):
        profile = profile + swapped(profile, step)
    return exposure, jnp.where(odd == 1, profile, to_even(profile))


def solution(mesh):
    return jax.shard_map(
        local,
        mesh=mesh,
        in_specs=(P("date", None, "path"), P("date", None, "path"), P(), P(), P(), P(), P()),
        out_specs=(P("date", None, "path"), P("date", None)),
        check_vma=False,
    )
```

```python
import functools

import jax
import jax.numpy as jnp
from jax import lax
from jax.experimental import pallas as pl
from jax.experimental.pallas import tpu as pltpu
from jax.sharding import PartitionSpec as P

LAG_MAX = 2
ridge_weight = 0.05
COS_TERMS = (
    1.4142124652862549,
    -27.915136337280273,
    91.82308197021484,
    -120.5933837890625,
    83.14732360839844,
    -29.807071685791016,
)
ROUNDER = 12582912.0
INV_TWO_PI = 0.15915494309189535
CHUNK = 512


def three_parts(x):
    hi = x.astype(jnp.bfloat16)
    rest = x - hi.astype(jnp.float32)
    mid = rest.astype(jnp.bfloat16)
    low = (rest - mid.astype(jnp.float32)).astype(jnp.bfloat16)
    return hi, mid, low


def turn_weights(freq_ref, phase_ref):
    r, k = freq_ref.shape
    rows = three_parts(freq_ref[...].astype(jnp.float32) * INV_TWO_PI)
    phase = three_parts(phase_ref[...] * INV_TWO_PI)
    rows = [part.astype(jnp.float32) for part in rows + phase]
    rest = jnp.zeros((r - len(phase), k), jnp.float32)
    return jnp.concatenate([*rows, rest], axis=0).T.astype(jnp.bfloat16)


def chunk_turns(weights, x):
    ones = jnp.ones(x.shape, jnp.bfloat16)
    return jnp.dot(
        weights, jnp.concatenate([x, x, x, ones], axis=0), preferred_element_type=jnp.float32
    )


def cosines(turns):
    part = turns - ((turns + ROUNDER) - ROUNDER)
    s = part * part
    total = jnp.full(s.shape, COS_TERMS[-1], jnp.float32)
    for term in COS_TERMS[-2::-1]:
        total = total * s + term
    return total.astype(jnp.bfloat16)


def features_kernel(freq_ref, phase_ref, factors_ref, features_ref):
    weights = turn_weights(freq_ref, phase_ref)
    for i in range(factors_ref.shape[0]):
        for at in range(0, factors_ref.shape[2], CHUNK):
            span = pl.ds(at, CHUNK)
            features_ref[i, :, span] = cosines(chunk_turns(weights, factors_ref[i, :, span]))


def sums_kernel(first_ref, freq_ref, phase_ref, factors_ref, flows_ref, *refs):
    (
        features_ref,
        sums_ref,
        freq_here,
        phase_here,
        factors_here,
        flows_here,
        features_here,
        weight_sems,
        factor_sems,
        flow_sems,
        feature_sems,
    ) = refs[-11:]
    dates, _, paths = factors_here.shape
    small = (
        pltpu.make_async_copy(freq_ref, freq_here, weight_sems.at[0]),
        pltpu.make_async_copy(phase_ref, phase_here, weight_sems.at[1]),
    )
    for copy in small:
        copy.start()
    loads, saves = [], []
    for i in range(dates):
        t = first_ref[0] + i
        loads.append(
            (
                pltpu.make_async_copy(factors_ref.at[t], factors_here.at[i], factor_sems.at[i]),
                pltpu.make_async_copy(flows_ref.at[t], flows_here.at[i], flow_sems.at[i]),
            )
        )
        saves.append(
            pltpu.make_async_copy(features_here.at[i], features_ref.at[t], feature_sems.at[i])
        )
        for copy in loads[-1]:
            copy.start()
    for copy in small:
        copy.wait()
    weights = turn_weights(freq_here, phase_here)
    items = [(i, pl.ds(at, CHUNK)) for i in range(dates) for at in range(0, paths, CHUNK)]
    arrived = set()

    def turns_of(item):
        i, span = item
        if i not in arrived:
            arrived.add(i)
            for copy in loads[i]:
                copy.wait()
        return chunk_turns(weights, factors_here[i, :, span])

    def product_of(item, feats):
        i, span = item
        both = jnp.concatenate([feats, flows_here[i, :, span]], axis=0)
        return lax.dot_general(
            both, feats, (((1,), (1,)), ((), ())), preferred_element_type=jnp.float32
        )

    turns, feats, sums = turns_of(items[0]), None, None
    for at in range(len(items) + 1):
        later = turns_of(items[at + 1]) if at + 1 < len(items) else None
        if at:
            i = items[at - 1][0]
            product = product_of(items[at - 1], feats)
            starts = at == 1 or items[at - 2][0] != i
            sums = product if starts else sums + product
            if at == len(items) or items[at][0] != i:
                sums_ref[i] = sums
                saves[i].start()
        if at < len(items):
            i, span = items[at]
            feats = cosines(turns)
            features_here[i, :, span] = feats
            turns = later
    for copy in saves:
        copy.wait()


ON_CHIP = pl.BlockSpec(memory_space=pltpu.VMEM)
SCALARS = pl.BlockSpec(memory_space=pltpu.SMEM)
IN_HBM = pl.BlockSpec(memory_space=pltpu.HBM)


def in_hbm(a):
    return pltpu.with_memory_space_constraint(a, pltpu.HBM)


def params(mebibytes):
    return pltpu.CompilerParams(vmem_limit_bytes=mebibytes << 20)


def features_of(frequency, phases, factors):
    dates, r, paths = factors.shape
    k = frequency.shape[1]
    return pl.pallas_call(
        features_kernel,
        in_specs=[ON_CHIP, ON_CHIP, ON_CHIP],
        out_specs=ON_CHIP,
        out_shape=jax.ShapeDtypeStruct((dates, k, paths), jnp.bfloat16),
        compiler_params=params(8),
        cost_estimate=pl.CostEstimate(
            flops=2000 * dates * k * paths, bytes_accessed=2 * dates * k * paths, transcendentals=0
        ),
        name="features",
    )(frequency, phases, factors)


def sums_of(first, dates, frequency, phases, factors, flows, features=None):
    dates_all, r, paths = factors.shape
    k, sets = frequency.shape[1], flows.shape[1]
    args = [first.reshape(1), *map(in_hbm, (frequency, phases, factors, flows))]
    aliases = {}
    if features is not None:
        aliases[len(args)] = 0
        args.append(in_hbm(features))
    return pl.pallas_call(
        sums_kernel,
        in_specs=[SCALARS] + [IN_HBM] * (len(args) - 1),
        out_specs=(IN_HBM, ON_CHIP),
        out_shape=(
            pltpu.HBM((dates_all, k, paths), jnp.bfloat16),
            jax.ShapeDtypeStruct((dates, k + sets, k), jnp.float32),
        ),
        scratch_shapes=[
            pltpu.VMEM(frequency.shape, frequency.dtype),
            pltpu.VMEM(phases.shape, phases.dtype),
            pltpu.VMEM((dates, r, paths), jnp.bfloat16),
            pltpu.VMEM((dates, sets, paths), jnp.bfloat16),
            pltpu.VMEM((dates, k, paths), jnp.bfloat16),
            pltpu.SemaphoreType.DMA((2,)),
            pltpu.SemaphoreType.DMA((dates,)),
            pltpu.SemaphoreType.DMA((dates,)),
            pltpu.SemaphoreType.DMA((dates,)),
        ],
        input_output_aliases=aliases,
        compiler_params=params(24),
        cost_estimate=pl.CostEstimate(
            flops=20000 * dates * k * paths, bytes_accessed=4 * dates * k * paths, transcendentals=0
        ),
        name="sums",
    )(*args)


def solve_kernel(paths_all, one_ref, two_ref, out_ref):
    k = one_ref.shape[1]
    total = (one_ref[...] + two_ref[...]) / paths_all
    row_at = lax.broadcasted_iota(jnp.int32, (k, k), 0)
    lane_at = lax.broadcasted_iota(jnp.int32, (k, k), 1)
    system = total[:k] + jnp.where(row_at == lane_at, ridge_weight, 0.0)
    m = jnp.concatenate([system, total[k:]], axis=0)
    lane = lax.broadcasted_iota(jnp.int32, (1, k), 1)
    for j in range(k):
        top = j // 8 * 8
        row = m[j - (k + 64 - m.shape[0]) : j - (k + 64 - m.shape[0]) + 1, :]
        pivot = 1.0 / row[:, j : j + 1]
        scaled = jnp.where(lane == j, 1.0 - pivot, row * pivot)
        if (j + 1) % 8 == 0:
            m = m[8:, :]
        m = m - m[:, j : j + 1] * scaled
    out_ref[...] = m.astype(jnp.bfloat16)


def solved(one, two, paths_all):
    k = one.shape[1]
    sets = one.shape[0] - k
    return pl.pallas_call(
        functools.partial(solve_kernel, paths_all),
        in_specs=[ON_CHIP, ON_CHIP],
        out_specs=ON_CHIP,
        out_shape=jax.ShapeDtypeStruct((sets, k), jnp.bfloat16),
        compiler_params=params(8),
        name="solve",
    )(one, two)


def value_of(coefs, feats):
    return jnp.dot(coefs, feats, preferred_element_type=jnp.float32).astype(jnp.bfloat16)


def limits_of(lag_ref, threshold_ref, transfer_ref):
    def column(ref):
        return jnp.broadcast_to(ref[...], (128, ref.shape[1])).T

    offset = (column(threshold_ref) + column(transfer_ref)).astype(jnp.float32) / 100.0
    recent = jnp.where(column(lag_ref) == 1, 1.0, 0.0)
    times = CHUNK // 128
    return jnp.concatenate([offset] * times, axis=1), jnp.concatenate([recent] * times, axis=1) > 0.5


def exposed_of(v, last, before, offset, recent):
    lagged = jnp.where(recent, last.astype(jnp.float32), before.astype(jnp.float32))
    collateral = jnp.maximum(lagged - offset, 0.0)
    return jnp.maximum(v.astype(jnp.float32) - collateral, 0.0)


def by_lane(exposed):
    return sum(exposed[:, i : i + 128] for i in range(0, exposed.shape[1], 128))


def profile_of(totals, paths_all, dates):
    sets = next(iter(totals.values())).shape[0]
    lane = lax.broadcasted_iota(jnp.int32, (sets, 128), 1)
    sums = jnp.zeros((sets, 128), jnp.float32)
    for t, total in totals.items():
        here = jnp.sum(total, axis=1, keepdims=True) / paths_all
        sums = jnp.where(lane == t, here, sums)
    return sums.T[:dates]


def later_kernel(
    paths_all,
    lag_ref,
    threshold_ref,
    transfer_ref,
    coefs_ref,
    features_ref,
    exposure_ref,
    early_ref,
    profile_ref,
    features_here,
    values_ref,
    staged_ref,
    feature_sems,
    sems,
):
    dates, sets, paths = values_ref.shape
    spans = [pl.ds(at, CHUNK) for at in range(0, paths, CHUNK)]
    loads = [
        pltpu.make_async_copy(features_ref.at[t], features_here.at[t], feature_sems.at[t])
        for t in range(dates)
    ]
    for copy in loads:
        copy.start()
    offset, recent = limits_of(lag_ref, threshold_ref, transfer_ref)
    totals, copies = {}, []
    for t in range(dates):
        loads[t].wait()
        for span in spans:
            values_ref[t, :, span] = value_of(coefs_ref[t], features_here[t, :, span])
        if t < LAG_MAX:
            early_ref[t] = values_ref[t]
            continue
        totals[t] = jnp.zeros((sets, 128), jnp.float32)
        for span in spans:
            exposed = exposed_of(
                *(values_ref[t - back, :, span] for back in range(LAG_MAX + 1)), offset, recent
            )
            staged_ref[t - LAG_MAX, :, span] = exposed.astype(jnp.bfloat16)
            totals[t] += by_lane(exposed)
        at = t - LAG_MAX
        copies.append(pltpu.make_async_copy(staged_ref.at[at], exposure_ref.at[t], sems.at[at]))
        copies[-1].start()
    profile_ref[...] = profile_of(totals, paths_all, dates)
    for copy in copies:
        copy.wait()


def first_kernel(
    paths_all,
    lag_ref,
    threshold_ref,
    transfer_ref,
    prior_coefs_ref,
    prior_features_ref,
    early_ref,
    profile_in_ref,
    exposure_in_ref,
    exposure_ref,
    profile_ref,
    staged_ref,
    sems,
):
    del exposure_in_ref
    sets, paths = early_ref.shape[1:]
    offset, recent = limits_of(lag_ref, threshold_ref, transfer_ref)
    totals = {t: jnp.zeros((sets, 128), jnp.float32) for t in range(LAG_MAX)}
    for at in range(0, paths, CHUNK):
        span = pl.ds(at, CHUNK)
        v = [value_of(prior_coefs_ref[i], prior_features_ref[i, :, span]) for i in range(LAG_MAX)]
        for t in range(LAG_MAX):
            v.append(early_ref[t, :, span])
            exposed = exposed_of(v[-1], v[-2], v[-3], offset, recent)
            staged_ref[t, :, span] = exposed.astype(jnp.bfloat16)
            totals[t] += by_lane(exposed)
    copies = [
        pltpu.make_async_copy(staged_ref.at[t], exposure_ref.at[t], sems.at[t])
        for t in range(LAG_MAX)
    ]
    for copy in copies:
        copy.start()
    profile_ref[...] = profile_in_ref[...] + profile_of(totals, paths_all, profile_ref.shape[0])
    for copy in copies:
        copy.wait()


def later_exposures(limits, coefs, features, paths_all):
    dates, k, paths = features.shape
    sets = coefs.shape[1]
    return pl.pallas_call(
        functools.partial(later_kernel, paths_all),
        in_specs=[ON_CHIP] * (len(limits) + 1) + [IN_HBM],
        out_specs=(IN_HBM, ON_CHIP, ON_CHIP),
        out_shape=(
            pltpu.HBM((dates, sets, paths), jnp.bfloat16),
            jax.ShapeDtypeStruct((LAG_MAX, sets, paths), jnp.bfloat16),
            jax.ShapeDtypeStruct((dates, sets), jnp.float32),
        ),
        scratch_shapes=[
            pltpu.VMEM((dates, k, paths), jnp.bfloat16),
            pltpu.VMEM((dates, sets, paths), jnp.bfloat16),
            pltpu.VMEM((dates - LAG_MAX, sets, paths), jnp.bfloat16),
            pltpu.SemaphoreType.DMA((dates,)),
            pltpu.SemaphoreType.DMA((dates - LAG_MAX,)),
        ],
        compiler_params=params(32),
        cost_estimate=pl.CostEstimate(
            flops=200 * dates * k * sets * paths,
            bytes_accessed=2 * dates * (k + sets) * paths,
            transcendentals=0,
        ),
        name="later",
    )(*limits, coefs, in_hbm(features))


def first_exposures(limits, prior_coefs, prior_features, early, profile, exposure, paths_all):
    args = (*limits, prior_coefs, prior_features, early, profile, exposure)
    return pl.pallas_call(
        functools.partial(first_kernel, paths_all),
        in_specs=[ON_CHIP] * (len(args) - 1) + [IN_HBM],
        out_specs=(IN_HBM, ON_CHIP),
        out_shape=(
            pltpu.HBM(exposure.shape, exposure.dtype),
            jax.ShapeDtypeStruct(profile.shape, profile.dtype),
        ),
        scratch_shapes=[
            pltpu.VMEM(early.shape, jnp.bfloat16),
            pltpu.SemaphoreType.DMA((LAG_MAX,)),
        ],
        input_output_aliases={len(args) - 1: 0},
        compiler_params=params(12),
        name="first",
    )(*args)


CORE, ROW, NEAR, NEXT, FAR = 1, 2, 4, 8, 24


def swapped(value, step):
    return lax.ppermute(value, "path", [(i, i ^ step) for i in range(lax.axis_size("path"))])


def picked(value, at):
    return lax.dynamic_index_in_dim(value, at, 0, keepdims=False)


def doubled(value, step, bit):
    other = swapped(value, step)
    low = jnp.where(bit == 0, value, other)
    high = jnp.where(bit == 0, other, value)
    return jnp.concatenate([low, high], axis=0)


def from_earlier(value):
    length = lax.axis_size("date")
    return lax.ppermute(value, "date", [(i, i + 1) for i in range(length - 1)])


def local(factors, cashflows, frequency, phases, margin_lag, thresholds, transfer_min):
    paths_all = factors.shape[2] * lax.axis_size("path")
    me = lax.axis_index("path")
    core, row, near = me & 1, (me >> 1) & 1, (me >> 2) & 1
    half = factors.shape[0] // 2
    quarter = half // 2
    firsts = (half * (1 - core), half * core + quarter * (1 - row), half * core + quarter * row)
    prior_factors = from_earlier(factors[-LAG_MAX:])
    phases = phases.reshape(1, -1)
    frequency = frequency.T
    features, sums_a = sums_of(firsts[0], half, frequency, phases, factors, cashflows)
    from_core = swapped(sums_a, CORE).reshape(2, quarter, *sums_a.shape[1:])
    first_b, prior_factors = lax.optimization_barrier((firsts[1], prior_factors))
    features, sums_b = sums_of(
        first_b, quarter, frequency, phases, factors, cashflows, features
    )
    from_row = swapped(sums_b + picked(from_core, 1 - row), ROW)
    features, sums_c = sums_of(firsts[2], quarter, frequency, phases, factors, cashflows, features)
    kept = sums_c + picked(from_core, row) + from_row
    kept = picked(kept, near) + swapped(picked(kept, 1 - near), NEAR)
    kept = kept + swapped(kept, NEXT)
    prior_features = features_of(frequency, phases, prior_factors)
    kept, prior_features = lax.optimization_barrier((kept, prior_features))
    coefs = solved(kept, swapped(kept, FAR), paths_all)
    coefs = doubled(coefs[None], NEAR, near)
    coefs = doubled(coefs, ROW, row)
    coefs = doubled(coefs, CORE, core)
    prior_coefs = from_earlier(coefs[-LAG_MAX:])
    limits = tuple(a.reshape(1, -1) for a in (margin_lag, thresholds, transfer_min))
    exposure, early, profile = later_exposures(limits, coefs, features, paths_all)
    exposure, profile = first_exposures(
        limits, prior_coefs, prior_features, early, profile, exposure, paths_all
    )
    for step in (CORE, ROW, NEAR, NEXT, FAR):
        profile = profile + swapped(profile, step)
    return exposure, profile


def solution(mesh):
    return jax.shard_map(
        local,
        mesh=mesh,
        in_specs=(P("date", None, "path"), P("date", None, "path"), P(), P(), P(), P(), P()),
        out_specs=(P("date", None, "path"), P("date", None)),
        check_vma=False,
    )
```

```python
import functools

import jax
import jax.numpy as jnp
from jax import lax
from jax.experimental import pallas as pl
from jax.experimental.pallas import tpu as pltpu
from jax.sharding import PartitionSpec as P

LAG_MAX = 2
ridge_weight = 0.05
COS_TERMS = (
    1.4142124652862549,
    -27.915136337280273,
    91.82308197021484,
    -120.5933837890625,
    83.14732360839844,
    -29.807071685791016,
)
ROUNDER = 12582912.0
INV_TWO_PI = 0.15915494309189535
CHUNK = 512
BLOCK = 8


def three_parts(x):
    hi = x.astype(jnp.bfloat16)
    rest = x - hi.astype(jnp.float32)
    mid = rest.astype(jnp.bfloat16)
    low = (rest - mid.astype(jnp.float32)).astype(jnp.bfloat16)
    return hi, mid, low


def turn_weights(freq_ref, phase_ref):
    r, k = freq_ref.shape
    rows = three_parts(freq_ref[...].astype(jnp.float32) * INV_TWO_PI)
    phase = three_parts(phase_ref[...] * INV_TWO_PI)
    rows = [part.astype(jnp.float32) for part in rows + phase]
    rest = jnp.zeros((r - len(phase), k), jnp.float32)
    return jnp.concatenate([*rows, rest], axis=0).T.astype(jnp.bfloat16)


def chunk_turns(weights, x):
    ones = jnp.ones(x.shape, jnp.bfloat16)
    return jnp.dot(
        weights, jnp.concatenate([x, x, x, ones], axis=0), preferred_element_type=jnp.float32
    )


def cosines(turns):
    part = turns - ((turns + ROUNDER) - ROUNDER)
    s = part * part
    total = jnp.full(s.shape, COS_TERMS[-1], jnp.float32)
    for term in COS_TERMS[-2::-1]:
        total = total * s + term
    return total.astype(jnp.bfloat16)


def features_kernel(freq_ref, phase_ref, factors_ref, features_ref):
    weights = turn_weights(freq_ref, phase_ref)
    for i in range(factors_ref.shape[0]):
        for at in range(0, factors_ref.shape[2], CHUNK):
            span = pl.ds(at, CHUNK)
            features_ref[i, :, span] = cosines(chunk_turns(weights, factors_ref[i, :, span]))


def sums_kernel(first_ref, freq_ref, phase_ref, factors_ref, flows_ref, *refs):
    (
        features_ref,
        sums_ref,
        freq_here,
        phase_here,
        factors_here,
        flows_here,
        features_here,
        weight_sems,
        factor_sems,
        flow_sems,
        feature_sems,
    ) = refs[-11:]
    dates, _, paths = factors_here.shape
    small = (
        pltpu.make_async_copy(freq_ref, freq_here, weight_sems.at[0]),
        pltpu.make_async_copy(phase_ref, phase_here, weight_sems.at[1]),
    )
    for copy in small:
        copy.start()
    ats = [first_ref[0] + i for i in range(dates)]
    factor_loads = [
        pltpu.make_async_copy(factors_ref.at[t], factors_here.at[i], factor_sems.at[i])
        for i, t in enumerate(ats)
    ]
    flow_loads = [
        pltpu.make_async_copy(flows_ref.at[t], flows_here.at[i], flow_sems.at[i])
        for i, t in enumerate(ats)
    ]
    for pair in zip(factor_loads, flow_loads):
        for copy in pair:
            copy.start()
    for copy in small:
        copy.wait()
    weights = turn_weights(freq_here, phase_here)
    items = [(i, pl.ds(at, CHUNK)) for i in range(dates) for at in range(0, paths, CHUNK)]
    arrived, joined, saves = set(), set(), []

    def turns_of(item):
        i, span = item
        if i not in arrived:
            arrived.add(i)
            factor_loads[i].wait()
        return chunk_turns(weights, factors_here[i, :, span])

    def product_of(item, feats):
        i, span = item
        if i not in joined:
            joined.add(i)
            flow_loads[i].wait()
        both = jnp.concatenate([feats, flows_here[i, :, span]], axis=0)
        return lax.dot_general(
            both, feats, (((1,), (1,)), ((), ())), preferred_element_type=jnp.float32
        )

    turns, feats, sums = turns_of(items[0]), None, None
    for at in range(len(items) + 1):
        later = turns_of(items[at + 1]) if at + 1 < len(items) else None
        if at:
            i = items[at - 1][0]
            product = product_of(items[at - 1], feats)
            starts = at == 1 or items[at - 2][0] != i
            sums = product if starts else sums + product
            if at == len(items) or items[at][0] != i:
                sums_ref[i] = sums
        if at < len(items):
            i, span = items[at]
            feats = cosines(turns)
            features_here[i, :, span] = feats
            saves.append(
                pltpu.make_async_copy(
                    features_here.at[i, :, span],
                    features_ref.at[ats[i], :, span],
                    feature_sems.at[at],
                )
            )
            saves[-1].start()
            turns = later
    for copy in saves:
        copy.wait()


ON_CHIP = pl.BlockSpec(memory_space=pltpu.VMEM)
SCALARS = pl.BlockSpec(memory_space=pltpu.SMEM)
IN_HBM = pl.BlockSpec(memory_space=pltpu.HBM)


def in_hbm(a):
    return pltpu.with_memory_space_constraint(a, pltpu.HBM)


def params(mebibytes):
    return pltpu.CompilerParams(vmem_limit_bytes=mebibytes << 20)


def features_of(frequency, phases, factors):
    dates, r, paths = factors.shape
    k = frequency.shape[1]
    return pl.pallas_call(
        features_kernel,
        in_specs=[ON_CHIP, ON_CHIP, ON_CHIP],
        out_specs=ON_CHIP,
        out_shape=jax.ShapeDtypeStruct((dates, k, paths), jnp.bfloat16),
        compiler_params=params(8),
        cost_estimate=pl.CostEstimate(
            flops=2000 * dates * k * paths, bytes_accessed=2 * dates * k * paths, transcendentals=0
        ),
        name="features",
    )(frequency, phases, factors)


def sums_of(first, dates, frequency, phases, factors, flows, features=None):
    dates_all, r, paths = factors.shape
    k, sets = frequency.shape[1], flows.shape[1]
    args = [first.reshape(1), *map(in_hbm, (frequency, phases, factors, flows))]
    aliases = {}
    if features is not None:
        aliases[len(args)] = 0
        args.append(in_hbm(features))
    return pl.pallas_call(
        sums_kernel,
        in_specs=[SCALARS] + [IN_HBM] * (len(args) - 1),
        out_specs=(IN_HBM, ON_CHIP),
        out_shape=(
            pltpu.HBM((dates_all, k, paths), jnp.bfloat16),
            jax.ShapeDtypeStruct((dates, k + sets, k), jnp.float32),
        ),
        scratch_shapes=[
            pltpu.VMEM(frequency.shape, frequency.dtype),
            pltpu.VMEM(phases.shape, phases.dtype),
            pltpu.VMEM((dates, r, paths), jnp.bfloat16),
            pltpu.VMEM((dates, sets, paths), jnp.bfloat16),
            pltpu.VMEM((dates, k, paths), jnp.bfloat16),
            pltpu.SemaphoreType.DMA((2,)),
            pltpu.SemaphoreType.DMA((dates,)),
            pltpu.SemaphoreType.DMA((dates,)),
            pltpu.SemaphoreType.DMA((dates * (paths // CHUNK),)),
        ],
        input_output_aliases=aliases,
        compiler_params=params(24),
        cost_estimate=pl.CostEstimate(
            flops=20000 * dates * k * paths, bytes_accessed=4 * dates * k * paths, transcendentals=0
        ),
        name="sums",
    )(*args)


def solve_kernel(paths_all, one_ref, two_ref, out_ref):
    k = one_ref.shape[1]
    total = (one_ref[...] + two_ref[...]) / paths_all
    row_at = lax.broadcasted_iota(jnp.int32, (k, k), 0)
    lane_at = lax.broadcasted_iota(jnp.int32, (k, k), 1)
    system = total[:k] + jnp.where(row_at == lane_at, ridge_weight, 0.0)
    m = jnp.concatenate([system, total[k:]], axis=0)
    lane = lax.broadcasted_iota(jnp.int32, (1, k), 1)
    for j in range(0, k, BLOCK):
        pivots = [m[i : i + 1, :] for i in range(BLOCK)]
        entries = [
            [jnp.broadcast_to(row[:, j + i : j + i + 1], (1, k)) for i in range(BLOCK)]
            for row in pivots
        ]
        rows = [row - jnp.where(lane == j + i, 1.0, 0.0) for i, row in enumerate(pivots)]
        for p in range(BLOCK):
            inverse = 1.0 / entries[p][p]
            rows[p] = rows[p] * inverse
            for q in range(p + 1, BLOCK):
                entries[p][q] = entries[p][q] * inverse
            for i in range(BLOCK):
                if i != p:
                    rows[i] = rows[i] - entries[i][p] * rows[p]
                    for q in range(p + 1, BLOCK):
                        entries[i][q] = entries[i][q] - entries[i][p] * entries[p][q]
        m = m[BLOCK:]
        m = m - sum(m[:, j + i : j + i + 1] * rows[i] for i in range(BLOCK))
    out_ref[...] = m.astype(jnp.bfloat16)


def solved(one, two, paths_all):
    k = one.shape[1]
    sets = one.shape[0] - k
    return pl.pallas_call(
        functools.partial(solve_kernel, paths_all),
        in_specs=[ON_CHIP, ON_CHIP],
        out_specs=ON_CHIP,
        out_shape=jax.ShapeDtypeStruct((sets, k), jnp.bfloat16),
        compiler_params=params(8),
        name="solve",
    )(one, two)


def value_of(coefs, feats):
    return jnp.dot(coefs, feats, preferred_element_type=jnp.float32).astype(jnp.bfloat16)


def limits_of(lag_ref, threshold_ref, transfer_ref):
    def column(ref):
        return jnp.broadcast_to(ref[...], (128, ref.shape[1])).T

    offset = (column(threshold_ref) + column(transfer_ref)).astype(jnp.float32) / 100.0
    recent = jnp.where(column(lag_ref) == 1, 1.0, 0.0)
    times = CHUNK // 128
    return jnp.concatenate([offset] * times, axis=1), jnp.concatenate(
        [recent.astype(jnp.bfloat16)] * times, axis=1
    ) > 0.5


def exposed_of(v, last, before, offset, recent):
    lagged = jnp.where(recent, last, before).astype(jnp.float32)
    collateral = jnp.maximum(lagged - offset, 0.0)
    return jnp.maximum(v.astype(jnp.float32) - collateral, 0.0)


def by_lane(exposed):
    return sum(exposed[:, i : i + 128] for i in range(0, exposed.shape[1], 128))


def profile_of(totals, paths_all, dates):
    sets = next(iter(totals.values())).shape[0]
    lane = lax.broadcasted_iota(jnp.int32, (sets, 128), 1)
    sums = jnp.zeros((sets, 128), jnp.float32)
    for t, total in totals.items():
        here = jnp.sum(total, axis=1, keepdims=True) / paths_all
        sums = jnp.where(lane == t, here, sums)
    return sums.T[:dates]


def later_kernel(
    paths_all,
    lag_ref,
    threshold_ref,
    transfer_ref,
    coefs_ref,
    features_ref,
    exposure_ref,
    early_ref,
    profile_ref,
    features_here,
    values_ref,
    staged_ref,
    feature_sems,
    sems,
):
    dates, sets, paths = values_ref.shape
    spans = [pl.ds(at, CHUNK) for at in range(0, paths, CHUNK)]
    loads = [
        pltpu.make_async_copy(features_ref.at[t], features_here.at[t], feature_sems.at[t])
        for t in range(dates)
    ]
    for copy in loads:
        copy.start()
    offset, recent = limits_of(lag_ref, threshold_ref, transfer_ref)
    totals, copies = {}, []
    for t in range(dates):
        loads[t].wait()
        for span in spans:
            values_ref[t, :, span] = value_of(coefs_ref[t], features_here[t, :, span])
        if t < LAG_MAX:
            early_ref[t] = values_ref[t]
            continue
        totals[t] = jnp.zeros((sets, 128), jnp.float32)
        for span in spans:
            exposed = exposed_of(
                *(values_ref[t - back, :, span] for back in range(LAG_MAX + 1)), offset, recent
            )
            staged_ref[t - LAG_MAX, :, span] = exposed.astype(jnp.bfloat16)
            totals[t] += by_lane(exposed)
        at = t - LAG_MAX
        copies.append(pltpu.make_async_copy(staged_ref.at[at], exposure_ref.at[t], sems.at[at]))
        copies[-1].start()
    profile_ref[...] = profile_of(totals, paths_all, dates)
    for copy in copies:
        copy.wait()


def first_kernel(
    paths_all,
    lag_ref,
    threshold_ref,
    transfer_ref,
    prior_coefs_ref,
    prior_features_ref,
    early_ref,
    profile_in_ref,
    exposure_in_ref,
    exposure_ref,
    profile_ref,
    staged_ref,
    sems,
):
    del exposure_in_ref
    sets, paths = early_ref.shape[1:]
    offset, recent = limits_of(lag_ref, threshold_ref, transfer_ref)
    totals = {t: jnp.zeros((sets, 128), jnp.float32) for t in range(LAG_MAX)}
    for at in range(0, paths, CHUNK):
        span = pl.ds(at, CHUNK)
        v = [value_of(prior_coefs_ref[i], prior_features_ref[i, :, span]) for i in range(LAG_MAX)]
        for t in range(LAG_MAX):
            v.append(early_ref[t, :, span])
            exposed = exposed_of(v[-1], v[-2], v[-3], offset, recent)
            staged_ref[t, :, span] = exposed.astype(jnp.bfloat16)
            totals[t] += by_lane(exposed)
    copies = [
        pltpu.make_async_copy(staged_ref.at[t], exposure_ref.at[t], sems.at[t])
        for t in range(LAG_MAX)
    ]
    for copy in copies:
        copy.start()
    profile = profile_in_ref[...] + profile_of(totals, paths_all, profile_in_ref.shape[0])
    flat = jnp.concatenate([profile[t : t + 1] for t in range(profile.shape[0])], axis=1)
    profile_ref[...] = jnp.broadcast_to(flat[None], profile_ref.shape)
    for copy in copies:
        copy.wait()


def later_exposures(limits, coefs, features, paths_all):
    dates, k, paths = features.shape
    sets = coefs.shape[1]
    return pl.pallas_call(
        functools.partial(later_kernel, paths_all),
        in_specs=[ON_CHIP] * (len(limits) + 1) + [IN_HBM],
        out_specs=(IN_HBM, ON_CHIP, ON_CHIP),
        out_shape=(
            pltpu.HBM((dates, sets, paths), jnp.bfloat16),
            jax.ShapeDtypeStruct((LAG_MAX, sets, paths), jnp.bfloat16),
            jax.ShapeDtypeStruct((dates, sets), jnp.float32),
        ),
        scratch_shapes=[
            pltpu.VMEM((dates, k, paths), jnp.bfloat16),
            pltpu.VMEM((dates, sets, paths), jnp.bfloat16),
            pltpu.VMEM((dates - LAG_MAX, sets, paths), jnp.bfloat16),
            pltpu.SemaphoreType.DMA((dates,)),
            pltpu.SemaphoreType.DMA((dates - LAG_MAX,)),
        ],
        compiler_params=params(32),
        cost_estimate=pl.CostEstimate(
            flops=200 * dates * k * sets * paths,
            bytes_accessed=2 * dates * (k + sets) * paths,
            transcendentals=0,
        ),
        name="later",
    )(*limits, coefs, in_hbm(features))


def first_exposures(limits, prior_coefs, prior_features, early, profile, exposure, paths_all):
    args = (*limits, prior_coefs, prior_features, early, profile, exposure)
    return pl.pallas_call(
        functools.partial(first_kernel, paths_all),
        in_specs=[ON_CHIP] * (len(args) - 1) + [IN_HBM],
        out_specs=(IN_HBM, ON_CHIP),
        out_shape=(
            pltpu.HBM(exposure.shape, exposure.dtype),
            jax.ShapeDtypeStruct((lax.axis_size("path"), 1, profile.size), profile.dtype),
        ),
        scratch_shapes=[
            pltpu.VMEM(early.shape, jnp.bfloat16),
            pltpu.SemaphoreType.DMA((LAG_MAX,)),
        ],
        input_output_aliases={len(args) - 1: 0},
        compiler_params=params(12),
        name="first",
    )(*args)


def total_kernel(parts_ref, total_ref):
    flat = jnp.sum(parts_ref[...], axis=0)
    dates, sets = total_ref.shape
    for t in range(dates):
        total_ref[t : t + 1, :] = flat[:, t * sets : (t + 1) * sets]


def total_of(parts, shape):
    return pl.pallas_call(
        total_kernel,
        in_specs=[ON_CHIP],
        out_specs=ON_CHIP,
        out_shape=jax.ShapeDtypeStruct(shape, parts.dtype),
        name="total",
    )(parts)


CORE, ROW, NEAR, NEXT, FAR = 1, 2, 4, 8, 24


def swapped(value, step):
    return lax.ppermute(value, "path", [(i, i ^ step) for i in range(lax.axis_size("path"))])


def picked(value, at):
    return lax.dynamic_index_in_dim(value, at, 0, keepdims=False)


def doubled(value, step, bit):
    other = swapped(value, step)
    low = jnp.where(bit == 0, value, other)
    high = jnp.where(bit == 0, other, value)
    return jnp.concatenate([low, high], axis=0)


def from_earlier(value):
    length = lax.axis_size("date")
    return lax.ppermute(value, "date", [(i, i + 1) for i in range(length - 1)])


def local(factors, cashflows, frequency, phases, margin_lag, thresholds, transfer_min):
    paths_all = factors.shape[2] * lax.axis_size("path")
    me = lax.axis_index("path")
    core, row, near = me & 1, (me >> 1) & 1, (me >> 2) & 1
    half = factors.shape[0] // 2
    quarter = half // 2
    firsts = (half * (1 - core), half * core + quarter * (1 - row), half * core + quarter * row)
    prior_factors = from_earlier(factors[-LAG_MAX:])
    phases = phases.reshape(1, -1)
    frequency = frequency.T
    features, sums_a = sums_of(firsts[0], half, frequency, phases, factors, cashflows)
    from_core = swapped(sums_a, CORE).reshape(2, quarter, *sums_a.shape[1:])
    first_b, prior_factors = lax.optimization_barrier((firsts[1], prior_factors))
    features, sums_b = sums_of(
        first_b, quarter, frequency, phases, factors, cashflows, features
    )
    from_row = swapped(sums_b + picked(from_core, 1 - row), ROW)
    features, sums_c = sums_of(firsts[2], quarter, frequency, phases, factors, cashflows, features)
    kept = sums_c + picked(from_core, row) + from_row
    kept = picked(kept, near) + swapped(picked(kept, 1 - near), NEAR)
    kept = kept + swapped(kept, NEXT)
    prior_features = features_of(frequency, phases, prior_factors)
    kept, prior_features = lax.optimization_barrier((kept, prior_features))
    coefs = solved(kept, swapped(kept, FAR), paths_all)
    coefs = doubled(coefs[None], NEAR, near)
    coefs = doubled(coefs, ROW, row)
    coefs = doubled(coefs, CORE, core)
    prior_coefs = from_earlier(coefs[-LAG_MAX:])
    limits = tuple(a.reshape(1, -1) for a in (margin_lag, thresholds, transfer_min))
    exposure, early, profile = later_exposures(limits, coefs, features, paths_all)
    exposure, parts = first_exposures(
        limits, prior_coefs, prior_features, early, profile, exposure, paths_all
    )
    return exposure, total_of(lax.all_to_all(parts, "path", 0, 0, tiled=True), profile.shape)


def solution(mesh):
    return jax.shard_map(
        local,
        mesh=mesh,
        in_specs=(P("date", None, "path"), P("date", None, "path"), P(), P(), P(), P(), P()),
        out_specs=(P("date", None, "path"), P("date", None)),
        check_vma=False,
    )
```

```python
import functools

import jax
import jax.numpy as jnp
from jax import lax
from jax.experimental import pallas as pl
from jax.experimental.pallas import tpu as pltpu
from jax.sharding import PartitionSpec as P

LAG_MAX = 2
ridge_weight = 0.05
COS_TERMS = (
    1.4142124652862549,
    -27.915136337280273,
    91.82308197021484,
    -120.5933837890625,
    83.14732360839844,
    -29.807071685791016,
)
ROUNDER = 12582912.0
INV_TWO_PI = 0.15915494309189535
CHUNK = 512
BLOCK = 8


def three_parts(x):
    hi = x.astype(jnp.bfloat16)
    rest = x - hi.astype(jnp.float32)
    mid = rest.astype(jnp.bfloat16)
    low = (rest - mid.astype(jnp.float32)).astype(jnp.bfloat16)
    return hi, mid, low


def turn_weights(freq_ref, phase_ref):
    r, k = freq_ref.shape
    rows = three_parts(freq_ref[...].astype(jnp.float32) * INV_TWO_PI)
    phase = three_parts(phase_ref[...] * INV_TWO_PI)
    rows = [part.astype(jnp.float32) for part in rows + phase]
    rest = jnp.zeros((r - len(phase), k), jnp.float32)
    return jnp.concatenate([*rows, rest], axis=0).T.astype(jnp.bfloat16)


def chunk_turns(weights, x):
    ones = jnp.ones(x.shape, jnp.bfloat16)
    return jnp.dot(
        weights, jnp.concatenate([x, x, x, ones], axis=0), preferred_element_type=jnp.float32
    )


def cosines(turns):
    part = turns - ((turns + ROUNDER) - ROUNDER)
    s = part * part
    total = jnp.full(s.shape, COS_TERMS[-1], jnp.float32)
    for term in COS_TERMS[-2::-1]:
        total = total * s + term
    return total.astype(jnp.bfloat16)


def features_kernel(weights_ref, factors_ref, features_ref):
    for i in range(factors_ref.shape[0]):
        for at in range(0, factors_ref.shape[2], CHUNK):
            span = pl.ds(at, CHUNK)
            features_ref[i, :, span] = cosines(
                chunk_turns(weights_ref[...], factors_ref[i, :, span])
            )


def sums_kernel(first_ref, *refs):
    *given, factors_ref, flows_ref = refs[: -6 if len(refs) == 9 else -10]
    if len(given) == 1:
        features_ref, sums_ref, factors_here, flows_here, factor_sems, flow_sems = refs[-6:]
    else:
        features_ref, sums_ref, weights_out_ref, freq_here, phase_here = refs[-10:-5]
        factors_here, flows_here, factor_sems, flow_sems, weight_sems = refs[-5:]
        small = [
            pltpu.make_async_copy(source, here, weight_sems.at[i])
            for i, (source, here) in enumerate(zip(given, (freq_here, phase_here)))
        ]
        for copy in small:
            copy.start()
    dates, _, paths = features_ref.shape
    ats = [first_ref[0] + i for i in range(dates)]
    factor_loads = [
        pltpu.make_async_copy(factors_ref.at[t], factors_here.at[i], factor_sems.at[i])
        for i, t in enumerate(ats)
    ]
    flow_loads = [
        pltpu.make_async_copy(flows_ref.at[t], flows_here.at[i], flow_sems.at[i])
        for i, t in enumerate(ats)
    ]
    for pair in zip(factor_loads, flow_loads):
        for copy in pair:
            copy.start()
    if len(given) == 1:
        weights = given[0][...]
    else:
        for copy in small:
            copy.wait()
        weights = turn_weights(freq_here, phase_here)
        weights_out_ref[...] = weights
    items = [(i, pl.ds(at, CHUNK)) for i in range(dates) for at in range(0, paths, CHUNK)]
    arrived, joined = set(), set()

    def turns_of(item):
        i, span = item
        if i not in arrived:
            arrived.add(i)
            factor_loads[i].wait()
        return chunk_turns(weights, factors_here[i, :, span])

    def product_of(item, feats):
        i, span = item
        if i not in joined:
            joined.add(i)
            flow_loads[i].wait()
        both = jnp.concatenate([feats, flows_here[i, :, span]], axis=0)
        return lax.dot_general(
            both, feats, (((1,), (1,)), ((), ())), preferred_element_type=jnp.float32
        )

    turns, feats, sums = turns_of(items[0]), None, None
    for at in range(len(items) + 1):
        later = turns_of(items[at + 1]) if at + 1 < len(items) else None
        if at:
            i = items[at - 1][0]
            product = product_of(items[at - 1], feats)
            starts = at == 1 or items[at - 2][0] != i
            sums = product if starts else sums + product
            if at == len(items) or items[at][0] != i:
                sums_ref[i] = sums
        if at < len(items):
            i, span = items[at]
            feats = cosines(turns)
            features_ref[i, :, span] = feats
            turns = later


ON_CHIP = pl.BlockSpec(memory_space=pltpu.VMEM)
SCALARS = pl.BlockSpec(memory_space=pltpu.SMEM)
IN_HBM = pl.BlockSpec(memory_space=pltpu.HBM)


def in_hbm(a):
    return pltpu.with_memory_space_constraint(a, pltpu.HBM)


def params(mebibytes):
    return pltpu.CompilerParams(vmem_limit_bytes=mebibytes << 20)


def features_of(weights, factors):
    dates, r, paths = factors.shape
    k = weights.shape[0]
    return pl.pallas_call(
        features_kernel,
        in_specs=[ON_CHIP, ON_CHIP],
        out_specs=ON_CHIP,
        out_shape=jax.ShapeDtypeStruct((dates, k, paths), jnp.bfloat16),
        compiler_params=params(8),
        cost_estimate=pl.CostEstimate(
            flops=2000 * dates * k * paths, bytes_accessed=2 * dates * k * paths, transcendentals=0
        ),
        name="features",
    )(weights, factors)


def sums_of(first, dates, given, factors, flows):
    _, r, paths = factors.shape
    k, sets = given[0].shape[len(given) - 1], flows.shape[1]
    outs = [
        jax.ShapeDtypeStruct((dates, k, paths), jnp.bfloat16),
        jax.ShapeDtypeStruct((dates, k + sets, k), jnp.float32),
    ]
    scratch = [
        pltpu.VMEM((dates, r, paths), jnp.bfloat16),
        pltpu.VMEM((dates, sets, paths), jnp.bfloat16),
        pltpu.SemaphoreType.DMA((dates,)),
        pltpu.SemaphoreType.DMA((dates,)),
    ]
    specs = [ON_CHIP]
    if len(given) == 2:
        outs.append(jax.ShapeDtypeStruct((k, 4 * r), jnp.bfloat16))
        scratch = [pltpu.VMEM(a.shape, a.dtype) for a in given] + scratch
        scratch.append(pltpu.SemaphoreType.DMA((2,)))
        specs = [IN_HBM, IN_HBM]
        given = map(in_hbm, given)
    return pl.pallas_call(
        sums_kernel,
        in_specs=[SCALARS, *specs, IN_HBM, IN_HBM],
        out_specs=(ON_CHIP,) * len(outs),
        out_shape=tuple(outs),
        scratch_shapes=scratch,
        compiler_params=params(14),
        cost_estimate=pl.CostEstimate(
            flops=20000 * dates * k * paths,
            bytes_accessed=4 * dates * k * paths,
            transcendentals=0,
        ),
        name="sums",
    )(first.reshape(1), *given, in_hbm(factors), in_hbm(flows))


def solve_kernel(paths_all, one_ref, two_ref, out_ref):
    k = one_ref.shape[1]
    total = (one_ref[...] + two_ref[...]) / paths_all
    row_at = lax.broadcasted_iota(jnp.int32, (k, k), 0)
    lane_at = lax.broadcasted_iota(jnp.int32, (k, k), 1)
    system = total[:k] + jnp.where(row_at == lane_at, ridge_weight, 0.0)
    m = jnp.concatenate([system, total[k:]], axis=0)
    lane = lax.broadcasted_iota(jnp.int32, (1, k), 1)
    for j in range(0, k, BLOCK):
        pivots = [m[i : i + 1, :] for i in range(BLOCK)]
        entries = [
            [jnp.broadcast_to(row[:, j + i : j + i + 1], (1, k)) for i in range(BLOCK)]
            for row in pivots
        ]
        rows = [row - jnp.where(lane == j + i, 1.0, 0.0) for i, row in enumerate(pivots)]
        for p in range(BLOCK):
            inverse = 1.0 / entries[p][p]
            rows[p] = rows[p] * inverse
            for q in range(p + 1, BLOCK):
                entries[p][q] = entries[p][q] * inverse
            for i in range(BLOCK):
                if i != p:
                    rows[i] = rows[i] - entries[i][p] * rows[p]
                    for q in range(p + 1, BLOCK):
                        entries[i][q] = entries[i][q] - entries[i][p] * entries[p][q]
        m = m[BLOCK:]
        m = m - sum(m[:, j + i : j + i + 1] * rows[i] for i in range(BLOCK))
    out_ref[...] = m.astype(jnp.bfloat16)


def solved(one, two, paths_all):
    k = one.shape[1]
    sets = one.shape[0] - k
    return pl.pallas_call(
        functools.partial(solve_kernel, paths_all),
        in_specs=[ON_CHIP, ON_CHIP],
        out_specs=ON_CHIP,
        out_shape=jax.ShapeDtypeStruct((sets, k), jnp.bfloat16),
        compiler_params=params(8),
        name="solve",
    )(one, two)


def value_of(coefs, feats):
    return jnp.dot(coefs, feats, preferred_element_type=jnp.float32).astype(jnp.bfloat16)


def limits_of(lag_ref, threshold_ref, transfer_ref):
    def column(ref):
        return jnp.broadcast_to(ref[...], (128, ref.shape[1])).T

    offset = (column(threshold_ref) + column(transfer_ref)).astype(jnp.float32) / 100.0
    recent = jnp.where(column(lag_ref) == 1, 1.0, 0.0)
    times = CHUNK // 128
    return jnp.concatenate([offset] * times, axis=1), jnp.concatenate(
        [recent.astype(jnp.bfloat16)] * times, axis=1
    ) > 0.5


def exposed_of(v, last, before, offset, recent):
    lagged = jnp.where(recent, last, before).astype(jnp.float32)
    collateral = jnp.maximum(lagged - offset, 0.0)
    return jnp.maximum(v.astype(jnp.float32) - collateral, 0.0)


def by_lane(exposed):
    return sum(exposed[:, i : i + 128] for i in range(0, exposed.shape[1], 128))


def profile_of(totals, paths_all, dates):
    sets = next(iter(totals.values())).shape[0]
    lane = lax.broadcasted_iota(jnp.int32, (sets, 128), 1)
    sums = jnp.zeros((sets, 128), jnp.float32)
    for t, total in totals.items():
        here = jnp.sum(total, axis=1, keepdims=True) / paths_all
        sums = jnp.where(lane == t, here, sums)
    return sums.T[:dates]


def later_kernel(
    paths_all,
    parts,
    firsts_ref,
    lag_ref,
    threshold_ref,
    transfer_ref,
    coefs_ref,
    *refs,
):
    exposure_ref, early_ref, profile_ref, values_ref, staged_ref, sems = refs[parts:]
    dates, sets, paths = values_ref.shape
    spans = [pl.ds(at, CHUNK) for at in range(0, paths, CHUNK)]
    for part, features_ref in enumerate(refs[:parts]):
        for i in range(features_ref.shape[0]):
            t = firsts_ref[part] + i
            for span in spans:
                values_ref[t, :, span] = value_of(coefs_ref[t], features_ref[i, :, span])
    offset, recent = limits_of(lag_ref, threshold_ref, transfer_ref)
    totals, copies = {}, []
    for t in range(LAG_MAX, dates):
        totals[t] = jnp.zeros((sets, 128), jnp.float32)
        for span in spans:
            exposed = exposed_of(
                *(values_ref[t - back, :, span] for back in range(LAG_MAX + 1)), offset, recent
            )
            staged_ref[t - LAG_MAX, :, span] = exposed.astype(jnp.bfloat16)
            totals[t] += by_lane(exposed)
        at = t - LAG_MAX
        copies.append(pltpu.make_async_copy(staged_ref.at[at], exposure_ref.at[t], sems.at[at]))
        copies[-1].start()
    early_ref[...] = values_ref[:LAG_MAX]
    profile_ref[...] = profile_of(totals, paths_all, dates)
    for copy in copies:
        copy.wait()


def first_kernel(
    paths_all,
    lag_ref,
    threshold_ref,
    transfer_ref,
    prior_coefs_ref,
    prior_features_ref,
    early_ref,
    profile_in_ref,
    exposure_in_ref,
    exposure_ref,
    profile_ref,
    staged_ref,
    sems,
):
    del exposure_in_ref
    sets, paths = early_ref.shape[1:]
    offset, recent = limits_of(lag_ref, threshold_ref, transfer_ref)
    totals = {t: jnp.zeros((sets, 128), jnp.float32) for t in range(LAG_MAX)}
    for at in range(0, paths, CHUNK):
        span = pl.ds(at, CHUNK)
        v = [value_of(prior_coefs_ref[i], prior_features_ref[i, :, span]) for i in range(LAG_MAX)]
        for t in range(LAG_MAX):
            v.append(early_ref[t, :, span])
            exposed = exposed_of(v[-1], v[-2], v[-3], offset, recent)
            staged_ref[t, :, span] = exposed.astype(jnp.bfloat16)
            totals[t] += by_lane(exposed)
    copies = [
        pltpu.make_async_copy(staged_ref.at[t], exposure_ref.at[t], sems.at[t])
        for t in range(LAG_MAX)
    ]
    for copy in copies:
        copy.start()
    profile = profile_in_ref[...] + profile_of(totals, paths_all, profile_in_ref.shape[0])
    flat = jnp.concatenate([profile[t : t + 1] for t in range(profile.shape[0])], axis=1)
    profile_ref[...] = jnp.broadcast_to(flat[None], profile_ref.shape)
    for copy in copies:
        copy.wait()


def later_exposures(firsts, limits, coefs, parts, paths_all):
    dates, sets, k = coefs.shape
    paths = parts[0].shape[2]
    return pl.pallas_call(
        functools.partial(later_kernel, paths_all, len(parts)),
        in_specs=[SCALARS] + [ON_CHIP] * (len(limits) + 1 + len(parts)),
        out_specs=(IN_HBM, ON_CHIP, ON_CHIP),
        out_shape=(
            pltpu.HBM((dates, sets, paths), jnp.bfloat16),
            jax.ShapeDtypeStruct((LAG_MAX, sets, paths), jnp.bfloat16),
            jax.ShapeDtypeStruct((dates, sets), jnp.float32),
        ),
        scratch_shapes=[
            pltpu.VMEM((dates, sets, paths), jnp.bfloat16),
            pltpu.VMEM((dates - LAG_MAX, sets, paths), jnp.bfloat16),
            pltpu.SemaphoreType.DMA((dates - LAG_MAX,)),
        ],
        compiler_params=params(20),
        cost_estimate=pl.CostEstimate(
            flops=200 * dates * k * sets * paths,
            bytes_accessed=2 * dates * (k + sets) * paths,
            transcendentals=0,
        ),
        name="later",
    )(firsts, *limits, coefs, *parts)


def first_exposures(limits, prior_coefs, prior_features, early, profile, exposure, paths_all):
    args = (*limits, prior_coefs, prior_features, early, profile, exposure)
    return pl.pallas_call(
        functools.partial(first_kernel, paths_all),
        in_specs=[ON_CHIP] * (len(args) - 1) + [IN_HBM],
        out_specs=(IN_HBM, ON_CHIP),
        out_shape=(
            pltpu.HBM(exposure.shape, exposure.dtype),
            jax.ShapeDtypeStruct((lax.axis_size("path"), 1, profile.size), profile.dtype),
        ),
        scratch_shapes=[
            pltpu.VMEM(early.shape, jnp.bfloat16),
            pltpu.SemaphoreType.DMA((LAG_MAX,)),
        ],
        input_output_aliases={len(args) - 1: 0},
        compiler_params=params(12),
        name="first",
    )(*args)


def total_kernel(parts_ref, total_ref):
    flat = jnp.sum(parts_ref[...], axis=0)
    dates, sets = total_ref.shape
    for t in range(dates):
        total_ref[t : t + 1, :] = flat[:, t * sets : (t + 1) * sets]


def total_of(parts, shape):
    return pl.pallas_call(
        total_kernel,
        in_specs=[ON_CHIP],
        out_specs=ON_CHIP,
        out_shape=jax.ShapeDtypeStruct(shape, parts.dtype),
        name="total",
    )(parts)


CORE, ROW, NEAR, NEXT, FAR = 1, 2, 4, 8, 24


def swapped(value, step):
    return lax.ppermute(value, "path", [(i, i ^ step) for i in range(lax.axis_size("path"))])


def picked(value, low):
    return jnp.where(low, value[0], value[1])


def doubled(value, step, low):
    other = swapped(value, step)
    first = jnp.where(low, value, other)
    second = jnp.where(low, other, value)
    return jnp.concatenate([first, second], axis=0)


def from_earlier(value):
    length = lax.axis_size("date")
    return lax.ppermute(value, "date", [(i, i + 1) for i in range(length - 1)])


def local(factors, cashflows, frequency, phases, margin_lag, thresholds, transfer_min):
    paths_all = factors.shape[2] * lax.axis_size("path")
    me = lax.axis_index("path").astype(jnp.uint32)
    core, row, near = (((me >> bit) & 1).astype(jnp.int32) for bit in range(3))
    half = factors.shape[0] // 2
    quarter = half // 2
    firsts = (half * (1 - core), half * core + quarter * (1 - row), half * core + quarter * row)
    scalars = (*firsts, jnp.stack(firsts), core == 0, row == 0, near == 0)
    first_a, first_b, first_c, firsts, core_low, row_low, near_low = lax.optimization_barrier(
        scalars
    )
    prior_factors = from_earlier(factors[-LAG_MAX:])
    given = (frequency.T, phases.reshape(1, -1))
    part_a, sums_a, weights = sums_of(first_a, half, given, factors, cashflows)
    from_core = swapped(sums_a, CORE).reshape(2, quarter, *sums_a.shape[1:])
    first_b, prior_factors = lax.optimization_barrier((first_b, prior_factors))
    part_b, sums_b = sums_of(first_b, quarter, (weights,), factors, cashflows)
    from_row = swapped(sums_b + picked(from_core[::-1], row_low), ROW)
    part_c, sums_c = sums_of(first_c, quarter, (weights,), factors, cashflows)
    kept = sums_c + picked(from_core, row_low) + from_row
    kept = picked(kept, near_low) + swapped(picked(kept[::-1], near_low), NEAR)
    kept = kept + swapped(kept, NEXT)
    prior_features = features_of(weights, prior_factors)
    kept, prior_features = lax.optimization_barrier((kept, prior_features))
    coefs = solved(kept, swapped(kept, FAR), paths_all)
    coefs = doubled(coefs[None], NEAR, near_low)
    coefs = doubled(coefs, ROW, row_low)
    coefs = doubled(coefs, CORE, core_low)
    prior_coefs = from_earlier(coefs[-LAG_MAX:])
    limits = tuple(a.reshape(1, -1) for a in (margin_lag, thresholds, transfer_min))
    exposure, early, profile = later_exposures(
        firsts, limits, coefs, (part_a, part_b, part_c), paths_all
    )
    exposure, parts = first_exposures(
        limits, prior_coefs, prior_features, early, profile, exposure, paths_all
    )
    return exposure, total_of(lax.all_to_all(parts, "path", 0, 0, tiled=True), profile.shape)


def solution(mesh):
    return jax.shard_map(
        local,
        mesh=mesh,
        in_specs=(P("date", None, "path"), P("date", None, "path"), P(), P(), P(), P(), P()),
        out_specs=(P("date", None, "path"), P("date", None)),
        check_vma=False,
    )
```

```python
import functools

import jax
import jax.numpy as jnp
from jax import lax
from jax.experimental import pallas as pl
from jax.experimental.pallas import tpu as pltpu
from jax.sharding import PartitionSpec as P

LAG_MAX = 2
ridge_weight = 0.05
COS_TERMS = (
    1.4142124652862549,
    -27.915136337280273,
    91.82308197021484,
    -120.5933837890625,
    83.14732360839844,
    -29.807071685791016,
)
ROUNDER = 12582912.0
INV_TWO_PI = 0.15915494309189535
CHUNK = 512
PIECES = 2
BLOCK = 8


def three_parts(x):
    hi = x.astype(jnp.bfloat16)
    rest = x - hi.astype(jnp.float32)
    mid = rest.astype(jnp.bfloat16)
    low = (rest - mid.astype(jnp.float32)).astype(jnp.bfloat16)
    return hi, mid, low


def turn_weights(freq_ref, phase_ref):
    r, k = freq_ref.shape
    rows = three_parts(freq_ref[...].astype(jnp.float32) * INV_TWO_PI)
    phase = three_parts(phase_ref[...] * INV_TWO_PI)
    rows = [part.astype(jnp.float32) for part in rows + phase]
    rest = jnp.zeros((r - len(phase), k), jnp.float32)
    return jnp.concatenate([*rows, rest], axis=0).T.astype(jnp.bfloat16)


def chunk_turns(weights, x):
    ones = jnp.ones(x.shape, jnp.bfloat16)
    return jnp.dot(
        weights, jnp.concatenate([x, x, x, ones], axis=0), preferred_element_type=jnp.float32
    )


def cosines(turns):
    part = turns - ((turns + ROUNDER) - ROUNDER)
    s = part * part
    total = jnp.full(s.shape, COS_TERMS[-1], jnp.float32)
    for term in COS_TERMS[-2::-1]:
        total = total * s + term
    return total.astype(jnp.bfloat16)


def features_kernel(weights_ref, factors_ref, features_ref):
    for i in range(factors_ref.shape[0]):
        for at in range(0, factors_ref.shape[2], CHUNK):
            span = pl.ds(at, CHUNK)
            features_ref[i, :, span] = cosines(
                chunk_turns(weights_ref[...], factors_ref[i, :, span])
            )


def sums_kernel(first_ref, *refs):
    *given, factors_ref, flows_ref = refs[: -6 if len(refs) == 9 else -10]
    if len(given) == 1:
        features_ref, sums_ref, factors_here, flows_here, factor_sems, flow_sems = refs[-6:]
    else:
        features_ref, sums_ref, weights_out_ref, freq_here, phase_here = refs[-10:-5]
        factors_here, flows_here, factor_sems, flow_sems, weight_sems = refs[-5:]
        small = [
            pltpu.make_async_copy(source, here, weight_sems.at[i])
            for i, (source, here) in enumerate(zip(given, (freq_here, phase_here)))
        ]
        for copy in small:
            copy.start()
    dates, _, paths = features_ref.shape
    ats = [first_ref[0] + i for i in range(dates)]
    factor_loads = [
        pltpu.make_async_copy(factors_ref.at[t], factors_here.at[i], factor_sems.at[i])
        for i, t in enumerate(ats)
    ]
    flow_loads = [
        pltpu.make_async_copy(flows_ref.at[t], flows_here.at[i], flow_sems.at[i])
        for i, t in enumerate(ats)
    ]
    for pair in zip(factor_loads, flow_loads):
        for copy in pair:
            copy.start()
    if len(given) == 1:
        weights = given[0][...]
    else:
        for copy in small:
            copy.wait()
        weights = turn_weights(freq_here, phase_here)
        weights_out_ref[...] = weights
    items = [(i, pl.ds(at, CHUNK)) for i in range(dates) for at in range(0, paths, CHUNK)]
    arrived, joined = set(), set()

    def turns_of(item):
        i, span = item
        if i not in arrived:
            arrived.add(i)
            factor_loads[i].wait()
        return chunk_turns(weights, factors_here[i, :, span])

    def product_of(item, feats):
        i, span = item
        if i not in joined:
            joined.add(i)
            flow_loads[i].wait()
        both = jnp.concatenate([feats, flows_here[i, :, span]], axis=0)
        return lax.dot_general(
            both, feats, (((1,), (1,)), ((), ())), preferred_element_type=jnp.float32
        )

    turns, feats, sums = turns_of(items[0]), None, None
    for at in range(len(items) + 1):
        later = turns_of(items[at + 1]) if at + 1 < len(items) else None
        if at:
            i = items[at - 1][0]
            product = product_of(items[at - 1], feats)
            starts = at == 1 or items[at - 2][0] != i
            sums = product if starts else sums + product
            if at == len(items) or items[at][0] != i:
                sums_ref[i] = sums
        if at < len(items):
            i, span = items[at]
            feats = cosines(turns)
            features_ref[i, :, span] = feats
            turns = later


ON_CHIP = pl.BlockSpec(memory_space=pltpu.VMEM)
SCALARS = pl.BlockSpec(memory_space=pltpu.SMEM)
IN_HBM = pl.BlockSpec(memory_space=pltpu.HBM)


def in_hbm(a):
    return pltpu.with_memory_space_constraint(a, pltpu.HBM)


def params(mebibytes):
    return pltpu.CompilerParams(vmem_limit_bytes=mebibytes << 20)


def features_of(weights, factors):
    dates, r, paths = factors.shape
    k = weights.shape[0]
    return pl.pallas_call(
        features_kernel,
        in_specs=[ON_CHIP, ON_CHIP],
        out_specs=ON_CHIP,
        out_shape=jax.ShapeDtypeStruct((dates, k, paths), jnp.bfloat16),
        compiler_params=params(8),
        cost_estimate=pl.CostEstimate(
            flops=2000 * dates * k * paths, bytes_accessed=2 * dates * k * paths, transcendentals=0
        ),
        name="features",
    )(weights, factors)


def sums_of(first, dates, given, factors, flows):
    _, r, paths = factors.shape
    k, sets = given[0].shape[len(given) - 1], flows.shape[1]
    outs = [
        jax.ShapeDtypeStruct((dates, k, paths), jnp.bfloat16),
        jax.ShapeDtypeStruct((dates, k + sets, k), jnp.float32),
    ]
    scratch = [
        pltpu.VMEM((dates, r, paths), jnp.bfloat16),
        pltpu.VMEM((dates, sets, paths), jnp.bfloat16),
        pltpu.SemaphoreType.DMA((dates,)),
        pltpu.SemaphoreType.DMA((dates,)),
    ]
    specs = [ON_CHIP]
    if len(given) == 2:
        outs.append(jax.ShapeDtypeStruct((k, 4 * r), jnp.bfloat16))
        scratch = [pltpu.VMEM(a.shape, a.dtype) for a in given] + scratch
        scratch.append(pltpu.SemaphoreType.DMA((2,)))
        specs = [IN_HBM, IN_HBM]
        given = map(in_hbm, given)
    return pl.pallas_call(
        sums_kernel,
        in_specs=[SCALARS, *specs, IN_HBM, IN_HBM],
        out_specs=(ON_CHIP,) * len(outs),
        out_shape=tuple(outs),
        scratch_shapes=scratch,
        compiler_params=params(14),
        cost_estimate=pl.CostEstimate(
            flops=20000 * dates * k * paths,
            bytes_accessed=4 * dates * k * paths,
            transcendentals=0,
        ),
        name="sums",
    )(first.reshape(1), *given, in_hbm(factors), in_hbm(flows))


def solve_kernel(paths_all, one_ref, two_ref, out_ref):
    k = one_ref.shape[1]
    total = (one_ref[...] + two_ref[...]) / paths_all
    row_at = lax.broadcasted_iota(jnp.int32, (k, k), 0)
    lane_at = lax.broadcasted_iota(jnp.int32, (k, k), 1)
    system = total[:k] + jnp.where(row_at == lane_at, ridge_weight, 0.0)
    m = jnp.concatenate([system, total[k:]], axis=0)
    lane = lax.broadcasted_iota(jnp.int32, (1, k), 1)
    for j in range(0, k, BLOCK):
        pivots = [m[i : i + 1, :] for i in range(BLOCK)]
        entries = [
            [jnp.broadcast_to(row[:, j + i : j + i + 1], (1, k)) for i in range(BLOCK)]
            for row in pivots
        ]
        rows = [row - jnp.where(lane == j + i, 1.0, 0.0) for i, row in enumerate(pivots)]
        for p in range(BLOCK):
            inverse = 1.0 / entries[p][p]
            rows[p] = rows[p] * inverse
            for q in range(p + 1, BLOCK):
                entries[p][q] = entries[p][q] * inverse
            for i in range(BLOCK):
                if i != p:
                    rows[i] = rows[i] - entries[i][p] * rows[p]
                    for q in range(p + 1, BLOCK):
                        entries[i][q] = entries[i][q] - entries[i][p] * entries[p][q]
        m = m[BLOCK:]
        m = m - sum(m[:, j + i : j + i + 1] * rows[i] for i in range(BLOCK))
    out_ref[...] = m.astype(jnp.bfloat16)


def solved(one, two, paths_all):
    k = one.shape[1]
    sets = one.shape[0] - k
    return pl.pallas_call(
        functools.partial(solve_kernel, paths_all),
        in_specs=[ON_CHIP, ON_CHIP],
        out_specs=ON_CHIP,
        out_shape=jax.ShapeDtypeStruct((sets, k), jnp.bfloat16),
        compiler_params=params(8),
        name="solve",
    )(one, two)


def value_of(coefs, feats):
    return jnp.dot(coefs, feats, preferred_element_type=jnp.float32).astype(jnp.bfloat16)


def limits_of(lag_ref, threshold_ref, transfer_ref):
    def column(ref):
        return jnp.broadcast_to(ref[...], (128, ref.shape[1])).T

    offset = (column(threshold_ref) + column(transfer_ref)).astype(jnp.float32) / 100.0
    recent = jnp.where(column(lag_ref) == 1, 1.0, 0.0)
    times = CHUNK // 128
    return jnp.concatenate([offset] * times, axis=1), jnp.concatenate(
        [recent.astype(jnp.bfloat16)] * times, axis=1
    ) > 0.5


def exposed_of(v, last, before, offset, recent):
    lagged = jnp.where(recent, last, before).astype(jnp.float32)
    collateral = jnp.maximum(lagged - offset, 0.0)
    return jnp.maximum(v.astype(jnp.float32) - collateral, 0.0)


def by_lane(exposed):
    return sum(exposed[:, i : i + 128] for i in range(0, exposed.shape[1], 128))


def profile_of(totals, paths_all, dates):
    sets = next(iter(totals.values())).shape[0]
    lane = lax.broadcasted_iota(jnp.int32, (sets, 128), 1)
    sums = jnp.zeros((sets, 128), jnp.float32)
    for t, total in totals.items():
        here = jnp.sum(total, axis=1, keepdims=True) / paths_all
        sums = jnp.where(lane == t, here, sums)
    return sums.T[:dates]


def add_values(first_ref, coefs_ref, features_ref, values_ref):
    for i in range(features_ref.shape[0]):
        t = first_ref[0] + i
        for at in range(0, values_ref.shape[2], CHUNK):
            span = pl.ds(at, CHUNK)
            values_ref[t, :, span] = value_of(coefs_ref[i], features_ref[i, :, span])


def values_kernel(first_ref, coefs_ref, features_ref, *refs):
    add_values(first_ref, coefs_ref, features_ref, refs[-1])


def later_kernel(
    paths_all,
    first_ref,
    lag_ref,
    threshold_ref,
    transfer_ref,
    coefs_ref,
    features_ref,
    given_values_ref,
    exposure_ref,
    values_ref,
    profile_ref,
    staged_ref,
    sems,
):
    del given_values_ref
    add_values(first_ref, coefs_ref, features_ref, values_ref)
    dates, sets, paths = values_ref.shape
    offset, recent = limits_of(lag_ref, threshold_ref, transfer_ref)
    totals, copies = {}, []
    for t in range(LAG_MAX, dates):
        totals[t] = jnp.zeros((sets, 128), jnp.float32)
        for at in range(0, paths, CHUNK):
            span = pl.ds(at, CHUNK)
            exposed = exposed_of(
                *(values_ref[t - back, :, span] for back in range(LAG_MAX + 1)), offset, recent
            )
            staged_ref[t - LAG_MAX, :, span] = exposed.astype(jnp.bfloat16)
            totals[t] += by_lane(exposed)
        at = t - LAG_MAX
        copies.append(pltpu.make_async_copy(staged_ref.at[at], exposure_ref.at[t], sems.at[at]))
        copies[-1].start()
    profile_ref[...] = profile_of(totals, paths_all, dates)
    for copy in copies:
        copy.wait()


def first_kernel(
    paths_all,
    lag_ref,
    threshold_ref,
    transfer_ref,
    prior_coefs_ref,
    prior_features_ref,
    values_ref,
    profile_in_ref,
    exposure_in_ref,
    exposure_ref,
    profile_ref,
    staged_ref,
    sems,
):
    del exposure_in_ref
    sets, paths = values_ref.shape[1:]
    offset, recent = limits_of(lag_ref, threshold_ref, transfer_ref)
    totals = {t: jnp.zeros((sets, 128), jnp.float32) for t in range(LAG_MAX)}
    copies, piece = [], paths // PIECES
    for at in range(0, paths, CHUNK):
        span = pl.ds(at, CHUNK)
        v = [value_of(prior_coefs_ref[i], prior_features_ref[i, :, span]) for i in range(LAG_MAX)]
        for t in range(LAG_MAX):
            v.append(values_ref[t, :, span])
            exposed = exposed_of(v[-1], v[-2], v[-3], offset, recent)
            staged_ref[t, :, span] = exposed.astype(jnp.bfloat16)
            totals[t] += by_lane(exposed)
        if (at + CHUNK) % piece == 0:
            there = pl.ds(at + CHUNK - piece, piece)
            copies.append(
                pltpu.make_async_copy(
                    staged_ref.at[:, :, there],
                    exposure_ref.at[pl.ds(0, LAG_MAX), :, there],
                    sems.at[len(copies)],
                )
            )
            copies[-1].start()
    profile = profile_in_ref[...] + profile_of(totals, paths_all, profile_in_ref.shape[0])
    flat = jnp.concatenate([profile[t : t + 1] for t in range(profile.shape[0])], axis=1)
    profile_ref[...] = jnp.broadcast_to(flat[None], profile_ref.shape)
    for copy in copies:
        copy.wait()


def values_of(first, coefs, features, dates, values=None):
    here, sets, k = coefs.shape
    paths = features.shape[2]
    given = () if values is None else (values,)
    return pl.pallas_call(
        values_kernel,
        in_specs=[SCALARS] + [ON_CHIP] * (2 + len(given)),
        out_specs=ON_CHIP,
        out_shape=jax.ShapeDtypeStruct((dates, sets, paths), jnp.bfloat16),
        input_output_aliases={3: 0} if given else {},
        compiler_params=params(4),
        cost_estimate=pl.CostEstimate(
            flops=200 * here * k * sets * paths,
            bytes_accessed=2 * here * (k + sets) * paths,
            transcendentals=0,
        ),
        name="values",
    )(first.reshape(1), coefs, features, *given)


def later_exposures(first, limits, coefs, features, values, paths_all):
    dates, sets, paths = values.shape
    args = (first.reshape(1), *limits, coefs, features, values)
    return pl.pallas_call(
        functools.partial(later_kernel, paths_all),
        in_specs=[SCALARS] + [ON_CHIP] * (len(args) - 1),
        out_specs=(IN_HBM, ON_CHIP, ON_CHIP),
        out_shape=(
            pltpu.HBM(values.shape, values.dtype),
            jax.ShapeDtypeStruct(values.shape, values.dtype),
            jax.ShapeDtypeStruct((dates, sets), jnp.float32),
        ),
        scratch_shapes=[
            pltpu.VMEM((dates - LAG_MAX, sets, paths), jnp.bfloat16),
            pltpu.SemaphoreType.DMA((dates - LAG_MAX,)),
        ],
        input_output_aliases={len(args) - 1: 1},
        compiler_params=params(12),
        cost_estimate=pl.CostEstimate(
            flops=200 * dates * 128 * sets * paths,
            bytes_accessed=4 * dates * sets * paths,
            transcendentals=0,
        ),
        name="later",
    )(*args)


def first_exposures(limits, prior_coefs, prior_features, values, profile, exposure, paths_all):
    args = (*limits, prior_coefs, prior_features, values, profile, exposure)
    return pl.pallas_call(
        functools.partial(first_kernel, paths_all),
        in_specs=[ON_CHIP] * (len(args) - 1) + [IN_HBM],
        out_specs=(IN_HBM, ON_CHIP),
        out_shape=(
            pltpu.HBM(exposure.shape, exposure.dtype),
            jax.ShapeDtypeStruct((lax.axis_size("path"), 1, profile.size), profile.dtype),
        ),
        scratch_shapes=[
            pltpu.VMEM((LAG_MAX, *values.shape[1:]), jnp.bfloat16),
            pltpu.SemaphoreType.DMA((PIECES,)),
        ],
        input_output_aliases={len(args) - 1: 0},
        compiler_params=params(8),
        name="first",
    )(*args)


def total_kernel(parts_ref, total_ref):
    flat = jnp.sum(parts_ref[...], axis=0)
    dates, sets = total_ref.shape
    for t in range(dates):
        total_ref[t : t + 1, :] = flat[:, t * sets : (t + 1) * sets]


def total_of(parts, shape):
    return pl.pallas_call(
        total_kernel,
        in_specs=[ON_CHIP],
        out_specs=ON_CHIP,
        out_shape=jax.ShapeDtypeStruct(shape, parts.dtype),
        name="total",
    )(pltpu.with_memory_space_constraint(parts, pltpu.VMEM))


CORE, ROW, NEAR, NEXT, FAR = 1, 2, 4, 8, 24


def swapped(value, step):
    return lax.ppermute(value, "path", [(i, i ^ step) for i in range(lax.axis_size("path"))])


def picked(value, low):
    return jnp.where(low, value[0], value[1])


def ordered(mine, other, low):
    first = jnp.where(low, mine, other)
    second = jnp.where(low, other, mine)
    return jnp.concatenate([first, second], axis=0)


def from_earlier(value):
    length = lax.axis_size("date")
    return lax.ppermute(value, "date", [(i, i + 1) for i in range(length - 1)])


def local(factors, cashflows, frequency, phases, margin_lag, thresholds, transfer_min):
    paths_all = factors.shape[2] * lax.axis_size("path")
    me = lax.axis_index("path").astype(jnp.uint32)
    core, row, near = (((me >> bit) & 1).astype(jnp.int32) for bit in range(3))
    half = factors.shape[0] // 2
    quarter = half // 2
    firsts = (half * (1 - core), half * core + quarter * (1 - row), half * core + quarter * row)
    first_a, first_b, first_c, core_low, row_low, near_low = lax.optimization_barrier(
        (*firsts, core == 0, row == 0, near == 0)
    )
    prior_factors = from_earlier(factors[-LAG_MAX:])
    given = (frequency.T, phases.reshape(1, -1))
    part_a, sums_a, weights = sums_of(first_a, half, given, factors, cashflows)
    from_core = swapped(sums_a, CORE).reshape(2, quarter, *sums_a.shape[1:])
    first_b, prior_factors = lax.optimization_barrier((first_b, prior_factors))
    part_b, sums_b = sums_of(first_b, quarter, (weights,), factors, cashflows)
    from_row = swapped(sums_b + picked(from_core[::-1], row_low), ROW)
    part_c, sums_c = sums_of(first_c, quarter, (weights,), factors, cashflows)
    kept = sums_c + picked(from_core, row_low) + from_row
    kept = picked(kept, near_low) + swapped(picked(kept[::-1], near_low), NEAR)
    kept = kept + swapped(kept, NEXT)
    prior_features = features_of(weights, prior_factors)
    kept, prior_features = lax.optimization_barrier((kept, prior_features))
    coefs = solved(kept, swapped(kept, FAR), paths_all)
    dates = factors.shape[0]
    coefs_c = ordered(coefs[None], swapped(coefs[None], NEAR), near_low)
    coefs_b = swapped(coefs_c, ROW)
    values = values_of(first_c, coefs_c, part_c, dates)
    coefs_here = ordered(coefs_c, coefs_b, row_low)
    coefs_a = swapped(coefs_here, CORE)
    values = values_of(first_b, coefs_b, part_b, dates, values)
    last_coefs = jnp.where(core_low, coefs_a[-LAG_MAX:], coefs_here[-LAG_MAX:])
    prior_coefs = from_earlier(last_coefs)
    limits = tuple(a.reshape(1, -1) for a in (margin_lag, thresholds, transfer_min))
    exposure, values, profile = later_exposures(
        first_a, limits, coefs_a, part_a, values, paths_all
    )
    exposure, parts = first_exposures(
        limits, prior_coefs, prior_features, values, profile, exposure, paths_all
    )
    return exposure, total_of(lax.all_to_all(parts, "path", 0, 0, tiled=True), profile.shape)


def solution(mesh):
    return jax.shard_map(
        local,
        mesh=mesh,
        in_specs=(P("date", None, "path"), P("date", None, "path"), P(), P(), P(), P(), P()),
        out_specs=(P("date", None, "path"), P("date", None)),
        check_vma=False,
    )
```

```python
import functools

import jax
import jax.numpy as jnp
from jax import lax
from jax.experimental import pallas as pl
from jax.experimental.pallas import tpu as pltpu
from jax.sharding import PartitionSpec as P

LAG_MAX = 2
ridge_weight = 0.05
COS_TERMS = (
    1.4142124652862549,
    -27.915136337280273,
    91.82308197021484,
    -120.5933837890625,
    83.14732360839844,
    -29.807071685791016,
)
ROUNDER = 12582912.0
INV_TWO_PI = 0.15915494309189535
CHUNK = 512
PIECES = 2
BLOCK = 8


def three_parts(x):
    hi = x.astype(jnp.bfloat16)
    rest = x - hi.astype(jnp.float32)
    mid = rest.astype(jnp.bfloat16)
    low = (rest - mid.astype(jnp.float32)).astype(jnp.bfloat16)
    return hi, mid, low


def turn_weights(freq_ref, phase_ref):
    r, k = freq_ref.shape
    rows = three_parts(freq_ref[...].astype(jnp.float32) * INV_TWO_PI)
    phase = three_parts(phase_ref[...] * INV_TWO_PI)
    rows = [part.astype(jnp.float32) for part in rows + phase]
    rest = jnp.zeros((r - len(phase), k), jnp.float32)
    return jnp.concatenate([*rows, rest], axis=0).T.astype(jnp.bfloat16)


def chunk_turns(weights, x):
    ones = jnp.ones(x.shape, jnp.bfloat16)
    return jnp.dot(
        weights, jnp.concatenate([x, x, x, ones], axis=0), preferred_element_type=jnp.float32
    )


def cosines(turns):
    part = turns - ((turns + ROUNDER) - ROUNDER)
    s = part * part
    total = jnp.full(s.shape, COS_TERMS[-1], jnp.float32)
    for term in COS_TERMS[-2::-1]:
        total = total * s + term
    return total.astype(jnp.bfloat16)


def features_kernel(weights_ref, factors_ref, features_ref):
    for i in range(factors_ref.shape[0]):
        for at in range(0, factors_ref.shape[2], CHUNK):
            span = pl.ds(at, CHUNK)
            features_ref[i, :, span] = cosines(
                chunk_turns(weights_ref[...], factors_ref[i, :, span])
            )


def packed(sums):
    k = sums.shape[1]
    half, quarter = k // 2, k // 4
    lane = lax.broadcasted_iota(jnp.int32, (quarter, k), 1)
    folded = jnp.where(lane < half, sums[:quarter], pltpu.roll(sums[quarter:half], half, 1))
    return jnp.concatenate([sums[k:], sums[half:k], folded], axis=0)


def unpacked(rows):
    k = rows.shape[1]
    half, quarter = k // 2, k // 4
    sets = rows.shape[0] - half - quarter
    low, folded = rows[sets : sets + half], rows[sets + half :]
    left = jnp.concatenate([folded, pltpu.roll(folded, half, 1)], axis=0)
    across = jnp.concatenate([left, low], axis=0).T[:half]
    lane = lax.broadcasted_iota(jnp.int32, (half, k), 1)
    return jnp.concatenate([jnp.where(lane < half, left, across), low], axis=0), rows[:sets]


def sums_kernel(first_ref, *refs):
    *given, factors_ref, flows_ref = refs[: -6 if len(refs) == 9 else -10]
    if len(given) == 1:
        features_ref, sums_ref, factors_here, flows_here, factor_sems, flow_sems = refs[-6:]
    else:
        features_ref, sums_ref, weights_out_ref, freq_here, phase_here = refs[-10:-5]
        factors_here, flows_here, factor_sems, flow_sems, weight_sems = refs[-5:]
        small = [
            pltpu.make_async_copy(source, here, weight_sems.at[i])
            for i, (source, here) in enumerate(zip(given, (freq_here, phase_here)))
        ]
        for copy in small:
            copy.start()
    dates, _, paths = features_ref.shape
    ats = [first_ref[0] + i for i in range(dates)]
    factor_loads = [
        pltpu.make_async_copy(factors_ref.at[t], factors_here.at[i], factor_sems.at[i])
        for i, t in enumerate(ats)
    ]
    flow_loads = [
        pltpu.make_async_copy(flows_ref.at[t], flows_here.at[i], flow_sems.at[i])
        for i, t in enumerate(ats)
    ]
    for pair in zip(factor_loads, flow_loads):
        for copy in pair:
            copy.start()
    if len(given) == 1:
        weights = given[0][...]
    else:
        for copy in small:
            copy.wait()
        weights = turn_weights(freq_here, phase_here)
        weights_out_ref[...] = weights
    items = [(i, pl.ds(at, CHUNK)) for i in range(dates) for at in range(0, paths, CHUNK)]
    arrived, joined = set(), set()

    def turns_of(item):
        i, span = item
        if i not in arrived:
            arrived.add(i)
            factor_loads[i].wait()
        return chunk_turns(weights, factors_here[i, :, span])

    def product_of(item, feats):
        i, span = item
        if i not in joined:
            joined.add(i)
            flow_loads[i].wait()
        both = jnp.concatenate([feats, flows_here[i, :, span]], axis=0)
        return lax.dot_general(
            both, feats, (((1,), (1,)), ((), ())), preferred_element_type=jnp.float32
        )

    turns, feats, sums = turns_of(items[0]), None, None
    for at in range(len(items) + 1):
        later = turns_of(items[at + 1]) if at + 1 < len(items) else None
        if at:
            i = items[at - 1][0]
            product = product_of(items[at - 1], feats)
            starts = at == 1 or items[at - 2][0] != i
            sums = product if starts else sums + product
            if at == len(items) or items[at][0] != i:
                sums_ref[i] = packed(sums)
        if at < len(items):
            i, span = items[at]
            feats = cosines(turns)
            features_ref[i, :, span] = feats
            turns = later


ON_CHIP = pl.BlockSpec(memory_space=pltpu.VMEM)
SCALARS = pl.BlockSpec(memory_space=pltpu.SMEM)
IN_HBM = pl.BlockSpec(memory_space=pltpu.HBM)


def in_hbm(a):
    return pltpu.with_memory_space_constraint(a, pltpu.HBM)


def params(mebibytes):
    return pltpu.CompilerParams(vmem_limit_bytes=mebibytes << 20)


def features_of(weights, factors):
    dates, r, paths = factors.shape
    k = weights.shape[0]
    return pl.pallas_call(
        features_kernel,
        in_specs=[ON_CHIP, ON_CHIP],
        out_specs=ON_CHIP,
        out_shape=jax.ShapeDtypeStruct((dates, k, paths), jnp.bfloat16),
        compiler_params=params(8),
        cost_estimate=pl.CostEstimate(
            flops=2000 * dates * k * paths, bytes_accessed=2 * dates * k * paths, transcendentals=0
        ),
        name="features",
    )(weights, factors)


def sums_of(first, dates, given, factors, flows):
    _, r, paths = factors.shape
    k, sets = given[0].shape[len(given) - 1], flows.shape[1]
    outs = [
        jax.ShapeDtypeStruct((dates, k, paths), jnp.bfloat16),
        jax.ShapeDtypeStruct((dates, sets + k // 2 + k // 4, k), jnp.float32),
    ]
    scratch = [
        pltpu.VMEM((dates, r, paths), jnp.bfloat16),
        pltpu.VMEM((dates, sets, paths), jnp.bfloat16),
        pltpu.SemaphoreType.DMA((dates,)),
        pltpu.SemaphoreType.DMA((dates,)),
    ]
    specs = [ON_CHIP]
    if len(given) == 2:
        outs.append(jax.ShapeDtypeStruct((k, 4 * r), jnp.bfloat16))
        scratch = [pltpu.VMEM(a.shape, a.dtype) for a in given] + scratch
        scratch.append(pltpu.SemaphoreType.DMA((2,)))
        specs = [IN_HBM, IN_HBM]
        given = map(in_hbm, given)
    return pl.pallas_call(
        sums_kernel,
        in_specs=[SCALARS, *specs, IN_HBM, IN_HBM],
        out_specs=(ON_CHIP,) * len(outs),
        out_shape=tuple(outs),
        scratch_shapes=scratch,
        compiler_params=params(14),
        cost_estimate=pl.CostEstimate(
            flops=20000 * dates * k * paths,
            bytes_accessed=4 * dates * k * paths,
            transcendentals=0,
        ),
        name="sums",
    )(first.reshape(1), *given, in_hbm(factors), in_hbm(flows))


def solve_kernel(paths_all, one_ref, two_ref, out_ref):
    k = one_ref.shape[1]
    system, right = unpacked((one_ref[...] + two_ref[...]) / paths_all)
    row_at = lax.broadcasted_iota(jnp.int32, (k, k), 0)
    lane_at = lax.broadcasted_iota(jnp.int32, (k, k), 1)
    system = system + jnp.where(row_at == lane_at, ridge_weight, 0.0)
    m = jnp.concatenate([system, right], axis=0)
    lane = lax.broadcasted_iota(jnp.int32, (1, k), 1)
    for j in range(0, k, BLOCK):
        pivots = [m[i : i + 1, :] for i in range(BLOCK)]
        entries = {
            (i, q): jnp.broadcast_to(pivots[i][:, j + q : j + q + 1], (1, k))
            for i in range(BLOCK)
            for q in range(i, BLOCK)
        }
        rows = [row - jnp.where(lane == j + i, 1.0, 0.0) for i, row in enumerate(pivots)]
        for p in range(BLOCK):
            inverse = 1.0 / entries[p, p]
            rows[p] = rows[p] * inverse
            scaled = {q: entries[p, q] * inverse for q in range(p + 1, BLOCK)}
            for i in range(BLOCK):
                if i != p:
                    factor = entries[min(i, p), max(i, p)]
                    rows[i] = rows[i] - factor * rows[p]
                    for q in range(max(i, p + 1), BLOCK):
                        entries[i, q] = entries[i, q] - factor * scaled[q]
            for q, entry in scaled.items():
                entries[p, q] = entry
        m = m[BLOCK:]
        m = m - sum(m[:, j + i : j + i + 1] * rows[i] for i in range(BLOCK))
    out_ref[...] = m.astype(jnp.bfloat16)


def solved(one, two, paths_all):
    k = one.shape[1]
    sets = one.shape[0] - k // 2 - k // 4
    return pl.pallas_call(
        functools.partial(solve_kernel, paths_all),
        in_specs=[ON_CHIP, ON_CHIP],
        out_specs=ON_CHIP,
        out_shape=jax.ShapeDtypeStruct((sets, k), jnp.bfloat16),
        compiler_params=params(8),
        name="solve",
    )(one, two)


def value_of(coefs, feats):
    return jnp.dot(coefs, feats, preferred_element_type=jnp.float32).astype(jnp.bfloat16)


def limits_of(lag_ref, threshold_ref, transfer_ref):
    def column(ref):
        return jnp.broadcast_to(ref[...], (128, ref.shape[1])).T

    offset = (column(threshold_ref) + column(transfer_ref)).astype(jnp.float32) / 100.0
    recent = jnp.where(column(lag_ref) == 1, 1.0, 0.0)
    times = CHUNK // 128
    return jnp.concatenate([offset] * times, axis=1), jnp.concatenate(
        [recent.astype(jnp.bfloat16)] * times, axis=1
    ) > 0.5


def exposed_of(v, last, before, offset, recent):
    lagged = jnp.where(recent, last, before).astype(jnp.float32)
    collateral = jnp.maximum(lagged - offset, 0.0)
    return jnp.maximum(v.astype(jnp.float32) - collateral, 0.0)


def by_lane(exposed):
    return sum(exposed[:, i : i + 128] for i in range(0, exposed.shape[1], 128))


def profile_of(totals, paths_all, dates):
    sets = next(iter(totals.values())).shape[0]
    lane = lax.broadcasted_iota(jnp.int32, (sets, 128), 1)
    sums = jnp.zeros((sets, 128), jnp.float32)
    for t, total in totals.items():
        here = jnp.sum(total, axis=1, keepdims=True) / paths_all
        sums = jnp.where(lane == t, here, sums)
    return sums.T[:dates]


def add_values(first_ref, coefs_ref, features_ref, values_ref):
    for i in range(features_ref.shape[0]):
        t = first_ref[0] + i
        for at in range(0, values_ref.shape[2], CHUNK):
            span = pl.ds(at, CHUNK)
            values_ref[t, :, span] = value_of(coefs_ref[i], features_ref[i, :, span])


def values_kernel(first_ref, coefs_ref, features_ref, *refs):
    add_values(first_ref, coefs_ref, features_ref, refs[-1])


def later_kernel(
    paths_all,
    first_ref,
    lag_ref,
    threshold_ref,
    transfer_ref,
    coefs_ref,
    features_ref,
    given_values_ref,
    exposure_ref,
    values_ref,
    profile_ref,
    staged_ref,
    sems,
):
    del given_values_ref
    add_values(first_ref, coefs_ref, features_ref, values_ref)
    dates, sets, paths = values_ref.shape
    offset, recent = limits_of(lag_ref, threshold_ref, transfer_ref)
    totals, copies = {}, []
    for t in range(LAG_MAX, dates):
        totals[t] = jnp.zeros((sets, 128), jnp.float32)
        for at in range(0, paths, CHUNK):
            span = pl.ds(at, CHUNK)
            exposed = exposed_of(
                *(values_ref[t - back, :, span] for back in range(LAG_MAX + 1)), offset, recent
            )
            staged_ref[t - LAG_MAX, :, span] = exposed.astype(jnp.bfloat16)
            totals[t] += by_lane(exposed)
        at = t - LAG_MAX
        copies.append(pltpu.make_async_copy(staged_ref.at[at], exposure_ref.at[t], sems.at[at]))
        copies[-1].start()
    profile_ref[...] = profile_of(totals, paths_all, dates)
    for copy in copies:
        copy.wait()


def first_kernel(
    paths_all,
    lag_ref,
    threshold_ref,
    transfer_ref,
    prior_coefs_ref,
    prior_features_ref,
    values_ref,
    profile_in_ref,
    exposure_in_ref,
    exposure_ref,
    profile_ref,
    staged_ref,
    sems,
):
    del exposure_in_ref
    sets, paths = values_ref.shape[1:]
    offset, recent = limits_of(lag_ref, threshold_ref, transfer_ref)
    totals = {t: jnp.zeros((sets, 128), jnp.float32) for t in range(LAG_MAX)}
    copies, piece = [], paths // PIECES
    for at in range(0, paths, CHUNK):
        span = pl.ds(at, CHUNK)
        v = [value_of(prior_coefs_ref[i], prior_features_ref[i, :, span]) for i in range(LAG_MAX)]
        for t in range(LAG_MAX):
            v.append(values_ref[t, :, span])
            exposed = exposed_of(v[-1], v[-2], v[-3], offset, recent)
            staged_ref[t, :, span] = exposed.astype(jnp.bfloat16)
            totals[t] += by_lane(exposed)
        if (at + CHUNK) % piece == 0:
            there = pl.ds(at + CHUNK - piece, piece)
            copies.append(
                pltpu.make_async_copy(
                    staged_ref.at[:, :, there],
                    exposure_ref.at[pl.ds(0, LAG_MAX), :, there],
                    sems.at[len(copies)],
                )
            )
            copies[-1].start()
    profile = profile_in_ref[...] + profile_of(totals, paths_all, profile_in_ref.shape[0])
    flat = jnp.concatenate([profile[t : t + 1] for t in range(profile.shape[0])], axis=1)
    profile_ref[...] = jnp.broadcast_to(flat[None], profile_ref.shape)
    for copy in copies:
        copy.wait()


def values_of(first, coefs, features, dates, values=None):
    here, sets, k = coefs.shape
    paths = features.shape[2]
    given = () if values is None else (values,)
    return pl.pallas_call(
        values_kernel,
        in_specs=[SCALARS] + [ON_CHIP] * (2 + len(given)),
        out_specs=ON_CHIP,
        out_shape=jax.ShapeDtypeStruct((dates, sets, paths), jnp.bfloat16),
        input_output_aliases={3: 0} if given else {},
        compiler_params=params(4),
        cost_estimate=pl.CostEstimate(
            flops=200 * here * k * sets * paths,
            bytes_accessed=2 * here * (k + sets) * paths,
            transcendentals=0,
        ),
        name="values",
    )(first.reshape(1), coefs, features, *given)


def later_exposures(first, limits, coefs, features, values, paths_all):
    dates, sets, paths = values.shape
    args = (first.reshape(1), *limits, coefs, features, values)
    return pl.pallas_call(
        functools.partial(later_kernel, paths_all),
        in_specs=[SCALARS] + [ON_CHIP] * (len(args) - 1),
        out_specs=(IN_HBM, ON_CHIP, ON_CHIP),
        out_shape=(
            pltpu.HBM(values.shape, values.dtype),
            jax.ShapeDtypeStruct(values.shape, values.dtype),
            jax.ShapeDtypeStruct((dates, sets), jnp.float32),
        ),
        scratch_shapes=[
            pltpu.VMEM((dates - LAG_MAX, sets, paths), jnp.bfloat16),
            pltpu.SemaphoreType.DMA((dates - LAG_MAX,)),
        ],
        input_output_aliases={len(args) - 1: 1},
        compiler_params=params(12),
        cost_estimate=pl.CostEstimate(
            flops=200 * dates * 128 * sets * paths,
            bytes_accessed=4 * dates * sets * paths,
            transcendentals=0,
        ),
        name="later",
    )(*args)


def first_exposures(limits, prior_coefs, prior_features, values, profile, exposure, paths_all):
    args = (*limits, prior_coefs, prior_features, values, profile, exposure)
    return pl.pallas_call(
        functools.partial(first_kernel, paths_all),
        in_specs=[ON_CHIP] * (len(args) - 1) + [IN_HBM],
        out_specs=(IN_HBM, ON_CHIP),
        out_shape=(
            pltpu.HBM(exposure.shape, exposure.dtype),
            jax.ShapeDtypeStruct((lax.axis_size("path"), 1, profile.size), profile.dtype),
        ),
        scratch_shapes=[
            pltpu.VMEM((LAG_MAX, *values.shape[1:]), jnp.bfloat16),
            pltpu.SemaphoreType.DMA((PIECES,)),
        ],
        input_output_aliases={len(args) - 1: 0},
        compiler_params=params(8),
        name="first",
    )(*args)


def total_kernel(parts_ref, total_ref):
    flat = jnp.sum(parts_ref[...], axis=0)
    dates, sets = total_ref.shape
    for t in range(dates):
        total_ref[t : t + 1, :] = flat[:, t * sets : (t + 1) * sets]


def total_of(parts, shape):
    return pl.pallas_call(
        total_kernel,
        in_specs=[ON_CHIP],
        out_specs=ON_CHIP,
        out_shape=jax.ShapeDtypeStruct(shape, parts.dtype),
        name="total",
    )(pltpu.with_memory_space_constraint(parts, pltpu.VMEM))


CORE, ROW, NEAR, NEXT, FAR = 1, 2, 4, 8, 24


def swapped(value, step):
    return lax.ppermute(value, "path", [(i, i ^ step) for i in range(lax.axis_size("path"))])


def picked(value, low):
    return jnp.where(low, value[0], value[1])


def ordered(mine, other, low):
    first = jnp.where(low, mine, other)
    second = jnp.where(low, other, mine)
    return jnp.concatenate([first, second], axis=0)


def from_earlier(value):
    length = lax.axis_size("date")
    return lax.ppermute(value, "date", [(i, i + 1) for i in range(length - 1)])


def local(factors, cashflows, frequency, phases, margin_lag, thresholds, transfer_min):
    paths_all = factors.shape[2] * lax.axis_size("path")
    me = lax.axis_index("path").astype(jnp.uint32)
    core, row, near = (((me >> bit) & 1).astype(jnp.int32) for bit in range(3))
    half = factors.shape[0] // 2
    quarter = half // 2
    firsts = (half * (1 - core), half * core + quarter * (1 - row), half * core + quarter * row)
    first_a, first_b, first_c, core_low, row_low, near_low = lax.optimization_barrier(
        (*firsts, core == 0, row == 0, near == 0)
    )
    prior_factors = from_earlier(factors[-LAG_MAX:])
    given = (frequency.T, phases.reshape(1, -1))
    part_a, sums_a, weights = sums_of(first_a, half, given, factors, cashflows)
    from_core = swapped(sums_a, CORE).reshape(2, quarter, *sums_a.shape[1:])
    first_b, prior_factors = lax.optimization_barrier((first_b, prior_factors))
    part_b, sums_b = sums_of(first_b, quarter, (weights,), factors, cashflows)
    from_row = swapped(sums_b + picked(from_core[::-1], row_low), ROW)
    part_c, sums_c = sums_of(first_c, quarter, (weights,), factors, cashflows)
    kept = sums_c + picked(from_core, row_low) + from_row
    kept = picked(kept, near_low) + swapped(picked(kept[::-1], near_low), NEAR)
    kept = kept + swapped(kept, NEXT)
    prior_features = features_of(weights, prior_factors)
    kept, prior_features = lax.optimization_barrier((kept, prior_features))
    coefs = solved(kept, swapped(kept, FAR), paths_all)
    dates = factors.shape[0]
    coefs_c = ordered(coefs[None], swapped(coefs[None], NEAR), near_low)
    coefs_b = swapped(coefs_c, ROW)
    values = values_of(first_c, coefs_c, part_c, dates)
    coefs_here = ordered(coefs_c, coefs_b, row_low)
    coefs_a = swapped(coefs_here, CORE)
    values = values_of(first_b, coefs_b, part_b, dates, values)
    last_coefs = jnp.where(core_low, coefs_a[-LAG_MAX:], coefs_here[-LAG_MAX:])
    prior_coefs = from_earlier(last_coefs)
    limits = tuple(a.reshape(1, -1) for a in (margin_lag, thresholds, transfer_min))
    exposure, values, profile = later_exposures(
        first_a, limits, coefs_a, part_a, values, paths_all
    )
    exposure, parts = first_exposures(
        limits, prior_coefs, prior_features, values, profile, exposure, paths_all
    )
    return exposure, total_of(lax.all_to_all(parts, "path", 0, 0, tiled=True), profile.shape)


def solution(mesh):
    return jax.shard_map(
        local,
        mesh=mesh,
        in_specs=(P("date", None, "path"), P("date", None, "path"), P(), P(), P(), P(), P()),
        out_specs=(P("date", None, "path"), P("date", None)),
        check_vma=False,
    )
```

```python
import functools

import jax
import jax.numpy as jnp
from jax import lax
from jax.experimental import pallas as pl
from jax.experimental.pallas import tpu as pltpu
from jax.sharding import PartitionSpec as P

LAG_MAX = 2
ridge_weight = 0.05
COS_TERMS = (
    1.4142124652862549,
    -27.915136337280273,
    91.82308197021484,
    -120.5933837890625,
    83.14732360839844,
    -29.807071685791016,
)
ROUNDER = 12582912.0
INV_TWO_PI = 0.15915494309189535
CHUNK = 512
PIECES = 4
BLOCK = 8


def three_parts(x):
    hi = x.astype(jnp.bfloat16)
    rest = x - hi.astype(jnp.float32)
    mid = rest.astype(jnp.bfloat16)
    low = (rest - mid.astype(jnp.float32)).astype(jnp.bfloat16)
    return hi, mid, low


def turn_weights(freq_ref, phase_ref):
    r, k = freq_ref.shape
    rows = three_parts(freq_ref[...].astype(jnp.float32) * INV_TWO_PI)
    phase = three_parts(phase_ref[...] * INV_TWO_PI)
    rows = [part.astype(jnp.float32) for part in rows + phase]
    rest = jnp.zeros((r - len(phase), k), jnp.float32)
    return jnp.concatenate([*rows, rest], axis=0).T.astype(jnp.bfloat16)


def chunk_turns(weights, x):
    ones = jnp.ones(x.shape, jnp.bfloat16)
    return jnp.dot(
        weights, jnp.concatenate([x, x, x, ones], axis=0), preferred_element_type=jnp.float32
    )


def cosines(turns):
    part = turns - ((turns + ROUNDER) - ROUNDER)
    s = part * part
    total = jnp.full(s.shape, COS_TERMS[-1], jnp.float32)
    for term in COS_TERMS[-2::-1]:
        total = total * s + term
    return total.astype(jnp.bfloat16)


def features_kernel(weights_ref, factors_ref, features_ref):
    for i in range(factors_ref.shape[0]):
        for at in range(0, factors_ref.shape[2], CHUNK):
            span = pl.ds(at, CHUNK)
            features_ref[i, :, span] = cosines(
                chunk_turns(weights_ref[...], factors_ref[i, :, span])
            )


def packed(sums):
    k = sums.shape[1]
    half, quarter = k // 2, k // 4
    lane = lax.broadcasted_iota(jnp.int32, (quarter, k), 1)
    folded = jnp.where(lane < half, sums[:quarter], pltpu.roll(sums[quarter:half], half, 1))
    return jnp.concatenate([sums[k:], sums[half:k], folded], axis=0)


def unpacked(rows):
    k = rows.shape[1]
    half, quarter = k // 2, k // 4
    sets = rows.shape[0] - half - quarter
    low, folded = rows[sets : sets + half], rows[sets + half :]
    left = jnp.concatenate([folded, pltpu.roll(folded, half, 1)], axis=0)
    across = jnp.concatenate([left, low], axis=0).T[:half]
    lane = lax.broadcasted_iota(jnp.int32, (half, k), 1)
    return jnp.concatenate([jnp.where(lane < half, left, across), low], axis=0), rows[:sets]


def sums_kernel(first_ref, *refs):
    *given, factors_ref, flows_ref = refs[: -6 if len(refs) == 9 else -10]
    if len(given) == 1:
        features_ref, sums_ref, factors_here, flows_here, factor_sems, flow_sems = refs[-6:]
    else:
        features_ref, sums_ref, weights_out_ref, freq_here, phase_here = refs[-10:-5]
        factors_here, flows_here, factor_sems, flow_sems, weight_sems = refs[-5:]
        small = [
            pltpu.make_async_copy(source, here, weight_sems.at[i])
            for i, (source, here) in enumerate(zip(given, (freq_here, phase_here)))
        ]
        for copy in small:
            copy.start()
    dates, _, paths = features_ref.shape
    ats = [first_ref[0] + i for i in range(dates)]
    factor_loads = [
        pltpu.make_async_copy(factors_ref.at[t], factors_here.at[i], factor_sems.at[i])
        for i, t in enumerate(ats)
    ]
    flow_loads = [
        pltpu.make_async_copy(flows_ref.at[t], flows_here.at[i], flow_sems.at[i])
        for i, t in enumerate(ats)
    ]
    for pair in zip(factor_loads, flow_loads):
        for copy in pair:
            copy.start()
    if len(given) == 1:
        weights = given[0][...]
    else:
        for copy in small:
            copy.wait()
        weights = turn_weights(freq_here, phase_here)
        weights_out_ref[...] = weights
    items = [(i, pl.ds(at, CHUNK)) for i in range(dates) for at in range(0, paths, CHUNK)]
    arrived, joined = set(), set()

    def turns_of(item):
        i, span = item
        if i not in arrived:
            arrived.add(i)
            factor_loads[i].wait()
        return chunk_turns(weights, factors_here[i, :, span])

    def product_of(item, feats):
        i, span = item
        if i not in joined:
            joined.add(i)
            flow_loads[i].wait()
        both = jnp.concatenate([feats, flows_here[i, :, span]], axis=0)
        return lax.dot_general(
            both, feats, (((1,), (1,)), ((), ())), preferred_element_type=jnp.float32
        )

    turns, feats, sums = turns_of(items[0]), None, None
    for at in range(len(items) + 1):
        later = turns_of(items[at + 1]) if at + 1 < len(items) else None
        if at:
            i = items[at - 1][0]
            product = product_of(items[at - 1], feats)
            starts = at == 1 or items[at - 2][0] != i
            sums = product if starts else sums + product
            if at == len(items) or items[at][0] != i:
                sums_ref[i] = packed(sums)
        if at < len(items):
            i, span = items[at]
            feats = cosines(turns)
            features_ref[i, :, span] = feats
            turns = later


ON_CHIP = pl.BlockSpec(memory_space=pltpu.VMEM)
SCALARS = pl.BlockSpec(memory_space=pltpu.SMEM)
IN_HBM = pl.BlockSpec(memory_space=pltpu.HBM)


def in_hbm(a):
    return pltpu.with_memory_space_constraint(a, pltpu.HBM)


def params(mebibytes):
    return pltpu.CompilerParams(vmem_limit_bytes=mebibytes << 20)


def features_of(weights, factors):
    dates, r, paths = factors.shape
    k = weights.shape[0]
    return pl.pallas_call(
        features_kernel,
        in_specs=[ON_CHIP, ON_CHIP],
        out_specs=ON_CHIP,
        out_shape=jax.ShapeDtypeStruct((dates, k, paths), jnp.bfloat16),
        compiler_params=params(8),
        cost_estimate=pl.CostEstimate(
            flops=2000 * dates * k * paths, bytes_accessed=2 * dates * k * paths, transcendentals=0
        ),
        name="features",
    )(weights, factors)


def sums_of(first, dates, given, factors, flows):
    _, r, paths = factors.shape
    k, sets = given[0].shape[len(given) - 1], flows.shape[1]
    outs = [
        jax.ShapeDtypeStruct((dates, k, paths), jnp.bfloat16),
        jax.ShapeDtypeStruct((dates, sets + k // 2 + k // 4, k), jnp.float32),
    ]
    scratch = [
        pltpu.VMEM((dates, r, paths), jnp.bfloat16),
        pltpu.VMEM((dates, sets, paths), jnp.bfloat16),
        pltpu.SemaphoreType.DMA((dates,)),
        pltpu.SemaphoreType.DMA((dates,)),
    ]
    specs = [ON_CHIP]
    if len(given) == 2:
        outs.append(jax.ShapeDtypeStruct((k, 4 * r), jnp.bfloat16))
        scratch = [pltpu.VMEM(a.shape, a.dtype) for a in given] + scratch
        scratch.append(pltpu.SemaphoreType.DMA((2,)))
        specs = [IN_HBM, IN_HBM]
        given = map(in_hbm, given)
    return pl.pallas_call(
        sums_kernel,
        in_specs=[SCALARS, *specs, IN_HBM, IN_HBM],
        out_specs=(ON_CHIP,) * len(outs),
        out_shape=tuple(outs),
        scratch_shapes=scratch,
        compiler_params=params(14),
        cost_estimate=pl.CostEstimate(
            flops=20000 * dates * k * paths,
            bytes_accessed=4 * dates * k * paths,
            transcendentals=0,
        ),
        name="sums",
    )(first.reshape(1), *given, in_hbm(factors), in_hbm(flows))


def solve_kernel(paths_all, one_ref, two_ref, out_ref):
    k = one_ref.shape[1]
    system, right = unpacked((one_ref[...] + two_ref[...]) / paths_all)
    row_at = lax.broadcasted_iota(jnp.int32, (k, k), 0)
    lane_at = lax.broadcasted_iota(jnp.int32, (k, k), 1)
    system = system + jnp.where(row_at == lane_at, ridge_weight, 0.0)
    m = jnp.concatenate([system, right], axis=0)
    lane = lax.broadcasted_iota(jnp.int32, (1, k), 1)
    for j in range(0, k, BLOCK):
        pivots = [m[i : i + 1, :] for i in range(BLOCK)]
        entries = {
            (i, q): jnp.broadcast_to(pivots[i][:, j + q : j + q + 1], (1, k))
            for i in range(BLOCK)
            for q in range(i, BLOCK)
        }
        rows = [row - jnp.where(lane == j + i, 1.0, 0.0) for i, row in enumerate(pivots)]
        for p in range(BLOCK):
            inverse = 1.0 / entries[p, p]
            rows[p] = rows[p] * inverse
            scaled = {q: entries[p, q] * inverse for q in range(p + 1, BLOCK)}
            for i in range(BLOCK):
                if i != p:
                    factor = entries[min(i, p), max(i, p)]
                    rows[i] = rows[i] - factor * rows[p]
                    for q in range(max(i, p + 1), BLOCK):
                        entries[i, q] = entries[i, q] - factor * scaled[q]
            for q, entry in scaled.items():
                entries[p, q] = entry
        m = m[BLOCK:]
        m = m - sum(m[:, j + i : j + i + 1] * rows[i] for i in range(BLOCK))
    out_ref[...] = m.astype(jnp.bfloat16)


def solved(one, two, paths_all):
    k = one.shape[1]
    sets = one.shape[0] - k // 2 - k // 4
    return pl.pallas_call(
        functools.partial(solve_kernel, paths_all),
        in_specs=[ON_CHIP, ON_CHIP],
        out_specs=ON_CHIP,
        out_shape=jax.ShapeDtypeStruct((sets, k), jnp.bfloat16),
        compiler_params=params(8),
        name="solve",
    )(one, two)


def value_of(coefs, feats):
    return jnp.dot(coefs, feats, preferred_element_type=jnp.float32).astype(jnp.bfloat16)


def limits_of(lag_ref, threshold_ref, transfer_ref):
    def column(ref):
        return jnp.broadcast_to(ref[...], (128, ref.shape[1])).T

    offset = (column(threshold_ref) + column(transfer_ref)).astype(jnp.float32) / 100.0
    recent = jnp.where(column(lag_ref) == 1, 1.0, 0.0)
    times = CHUNK // 128
    return jnp.concatenate([offset] * times, axis=1), jnp.concatenate(
        [recent.astype(jnp.bfloat16)] * times, axis=1
    ) > 0.5


def exposed_of(v, last, before, offset, recent):
    lagged = jnp.where(recent, last, before).astype(jnp.float32)
    collateral = jnp.maximum(lagged - offset, 0.0)
    return jnp.maximum(v.astype(jnp.float32) - collateral, 0.0)


def by_lane(exposed):
    return sum(exposed[:, i : i + 128] for i in range(0, exposed.shape[1], 128))


def profile_of(totals, paths_all, dates):
    sets = next(iter(totals.values())).shape[0]
    lane = lax.broadcasted_iota(jnp.int32, (sets, 128), 1)
    sums = jnp.zeros((sets, 128), jnp.float32)
    for t, total in totals.items():
        here = jnp.sum(total, axis=1, keepdims=True) / paths_all
        sums = jnp.where(lane == t, here, sums)
    return sums.T[:dates]


def add_values(first_ref, coefs_ref, features_ref, values_ref):
    for i in range(features_ref.shape[0]):
        t = first_ref[0] + i
        for at in range(0, values_ref.shape[2], CHUNK):
            span = pl.ds(at, CHUNK)
            values_ref[t, :, span] = value_of(coefs_ref[i], features_ref[i, :, span])


def values_kernel(first_ref, coefs_ref, features_ref, *refs):
    add_values(first_ref, coefs_ref, features_ref, refs[-1])


def later_kernel(
    paths_all,
    first_ref,
    lag_ref,
    threshold_ref,
    transfer_ref,
    coefs_ref,
    features_ref,
    given_values_ref,
    exposure_ref,
    values_ref,
    profile_ref,
    staged_ref,
    sems,
):
    del given_values_ref
    add_values(first_ref, coefs_ref, features_ref, values_ref)
    dates, sets, paths = values_ref.shape
    offset, recent = limits_of(lag_ref, threshold_ref, transfer_ref)
    totals, copies = {}, []
    for t in range(LAG_MAX, dates):
        totals[t] = jnp.zeros((sets, 128), jnp.float32)
        for at in range(0, paths, CHUNK):
            span = pl.ds(at, CHUNK)
            exposed = exposed_of(
                *(values_ref[t - back, :, span] for back in range(LAG_MAX + 1)), offset, recent
            )
            staged_ref[t - LAG_MAX, :, span] = exposed.astype(jnp.bfloat16)
            totals[t] += by_lane(exposed)
        at = t - LAG_MAX
        copies.append(pltpu.make_async_copy(staged_ref.at[at], exposure_ref.at[t], sems.at[at]))
        copies[-1].start()
    profile_ref[...] = profile_of(totals, paths_all, dates)
    for copy in copies:
        copy.wait()


def first_kernel(
    paths_all,
    lag_ref,
    threshold_ref,
    transfer_ref,
    prior_coefs_ref,
    prior_features_ref,
    values_ref,
    profile_in_ref,
    exposure_in_ref,
    exposure_ref,
    profile_ref,
    staged_ref,
    sems,
):
    del exposure_in_ref
    sets, paths = values_ref.shape[1:]
    offset, recent = limits_of(lag_ref, threshold_ref, transfer_ref)
    totals = {t: jnp.zeros((sets, 128), jnp.float32) for t in range(LAG_MAX)}
    copies, piece = [], paths // PIECES
    for at in range(0, paths, CHUNK):
        span = pl.ds(at, CHUNK)
        v = [value_of(prior_coefs_ref[i], prior_features_ref[i, :, span]) for i in range(LAG_MAX)]
        for t in range(LAG_MAX):
            v.append(values_ref[t, :, span])
            exposed = exposed_of(v[-1], v[-2], v[-3], offset, recent)
            staged_ref[t, :, span] = exposed.astype(jnp.bfloat16)
            totals[t] += by_lane(exposed)
        if (at + CHUNK) % piece == 0:
            there = pl.ds(at + CHUNK - piece, piece)
            copies.append(
                pltpu.make_async_copy(
                    staged_ref.at[:, :, there],
                    exposure_ref.at[pl.ds(0, LAG_MAX), :, there],
                    sems.at[len(copies)],
                )
            )
            copies[-1].start()
    profile = profile_in_ref[...] + profile_of(totals, paths_all, profile_in_ref.shape[0])
    flat = jnp.concatenate([profile[t : t + 1] for t in range(profile.shape[0])], axis=1)
    profile_ref[...] = jnp.broadcast_to(flat[None], profile_ref.shape)
    for copy in copies:
        copy.wait()


def values_of(first, coefs, features, dates, values=None):
    here, sets, k = coefs.shape
    paths = features.shape[2]
    given = () if values is None else (values,)
    return pl.pallas_call(
        values_kernel,
        in_specs=[SCALARS] + [ON_CHIP] * (2 + len(given)),
        out_specs=ON_CHIP,
        out_shape=jax.ShapeDtypeStruct((dates, sets, paths), jnp.bfloat16),
        input_output_aliases={3: 0} if given else {},
        compiler_params=params(4),
        cost_estimate=pl.CostEstimate(
            flops=200 * here * k * sets * paths,
            bytes_accessed=2 * here * (k + sets) * paths,
            transcendentals=0,
        ),
        name="values",
    )(first.reshape(1), coefs, features, *given)


def later_exposures(first, limits, coefs, features, values, paths_all):
    dates, sets, paths = values.shape
    args = (first.reshape(1), *limits, coefs, features, values)
    return pl.pallas_call(
        functools.partial(later_kernel, paths_all),
        in_specs=[SCALARS] + [ON_CHIP] * (len(args) - 1),
        out_specs=(IN_HBM, ON_CHIP, ON_CHIP),
        out_shape=(
            pltpu.HBM(values.shape, values.dtype),
            jax.ShapeDtypeStruct(values.shape, values.dtype),
            jax.ShapeDtypeStruct((dates, sets), jnp.float32),
        ),
        scratch_shapes=[
            pltpu.VMEM((dates - LAG_MAX, sets, paths), jnp.bfloat16),
            pltpu.SemaphoreType.DMA((dates - LAG_MAX,)),
        ],
        input_output_aliases={len(args) - 1: 1},
        compiler_params=params(12),
        cost_estimate=pl.CostEstimate(
            flops=200 * dates * 128 * sets * paths,
            bytes_accessed=4 * dates * sets * paths,
            transcendentals=0,
        ),
        name="later",
    )(*args)


def first_exposures(limits, prior_coefs, prior_features, values, profile, exposure, paths_all):
    args = (*limits, prior_coefs, prior_features, values, profile, exposure)
    return pl.pallas_call(
        functools.partial(first_kernel, paths_all),
        in_specs=[ON_CHIP] * (len(args) - 1) + [IN_HBM],
        out_specs=(IN_HBM, ON_CHIP),
        out_shape=(
            pltpu.HBM(exposure.shape, exposure.dtype),
            jax.ShapeDtypeStruct((lax.axis_size("path"), 1, profile.size), profile.dtype),
        ),
        scratch_shapes=[
            pltpu.VMEM((LAG_MAX, *values.shape[1:]), jnp.bfloat16),
            pltpu.SemaphoreType.DMA((PIECES,)),
        ],
        input_output_aliases={len(args) - 1: 0},
        compiler_params=params(8),
        name="first",
    )(*args)


def total_kernel(parts_ref, total_ref):
    flat = jnp.sum(parts_ref[...], axis=0)
    dates, sets = total_ref.shape
    for t in range(dates):
        total_ref[t : t + 1, :] = flat[:, t * sets : (t + 1) * sets]


def total_of(parts, shape):
    return pl.pallas_call(
        total_kernel,
        in_specs=[ON_CHIP],
        out_specs=ON_CHIP,
        out_shape=jax.ShapeDtypeStruct(shape, parts.dtype),
        name="total",
    )(pltpu.with_memory_space_constraint(parts, pltpu.VMEM))


CORE, ROW, NEAR, NEXT, FAR = 1, 2, 4, 8, 24


def swapped(value, step):
    return lax.ppermute(value, "path", [(i, i ^ step) for i in range(lax.axis_size("path"))])


def picked(value, low):
    return jnp.where(low, value[0], value[1])


def ordered(mine, other, low):
    first = jnp.where(low, mine, other)
    second = jnp.where(low, other, mine)
    return jnp.concatenate([first, second], axis=0)


def from_earlier(value):
    length = lax.axis_size("date")
    return lax.ppermute(value, "date", [(i, i + 1) for i in range(length - 1)])


def local(factors, cashflows, frequency, phases, margin_lag, thresholds, transfer_min):
    paths_all = factors.shape[2] * lax.axis_size("path")
    me = lax.axis_index("path").astype(jnp.uint32)
    core, row, near = (((me >> bit) & 1).astype(jnp.int32) for bit in range(3))
    half = factors.shape[0] // 2
    quarter = half // 2
    firsts = (half * (1 - core), half * core + quarter * (1 - row), half * core + quarter * row)
    first_a, first_b, first_c, core_low, row_low, near_low = lax.optimization_barrier(
        (*firsts, core == 0, row == 0, near == 0)
    )
    prior_factors = from_earlier(factors[-LAG_MAX:])
    given = (frequency.T, phases.reshape(1, -1))
    part_a, sums_a, weights = sums_of(first_a, half, given, factors, cashflows)
    from_core = swapped(sums_a, CORE).reshape(2, quarter, *sums_a.shape[1:])
    first_b, prior_factors = lax.optimization_barrier((first_b, prior_factors))
    part_b, sums_b = sums_of(first_b, quarter, (weights,), factors, cashflows)
    from_row = swapped(sums_b + picked(from_core[::-1], row_low), ROW)
    part_c, sums_c = sums_of(first_c, quarter, (weights,), factors, cashflows)
    kept = sums_c + picked(from_core, row_low) + from_row
    kept = picked(kept, near_low) + swapped(picked(kept[::-1], near_low), NEAR)
    kept = kept + swapped(kept, NEXT)
    prior_features = features_of(weights, prior_factors)
    from_far, prior_features = lax.optimization_barrier((swapped(kept, FAR), prior_features))
    coefs = solved(kept, from_far, paths_all)
    dates = factors.shape[0]
    coefs_c = ordered(coefs[None], swapped(coefs[None], NEAR), near_low)
    coefs_b = swapped(coefs_c, ROW)
    values = values_of(first_c, coefs_c, part_c, dates)
    coefs_here = ordered(coefs_c, coefs_b, row_low)
    coefs_a = swapped(coefs_here, CORE)
    values = values_of(first_b, coefs_b, part_b, dates, values)
    last_coefs = jnp.where(core_low, coefs_a[-LAG_MAX:], coefs_here[-LAG_MAX:])
    prior_coefs = from_earlier(last_coefs)
    limits = tuple(a.reshape(1, -1) for a in (margin_lag, thresholds, transfer_min))
    exposure, values, profile = later_exposures(
        first_a, limits, coefs_a, part_a, values, paths_all
    )
    exposure, parts = first_exposures(
        limits, prior_coefs, prior_features, values, profile, exposure, paths_all
    )
    return exposure, total_of(lax.all_to_all(parts, "path", 0, 0, tiled=True), profile.shape)


def solution(mesh):
    return jax.shard_map(
        local,
        mesh=mesh,
        in_specs=(P("date", None, "path"), P("date", None, "path"), P(), P(), P(), P(), P()),
        out_specs=(P("date", None, "path"), P("date", None)),
        check_vma=False,
    )
```

```python
import functools

import jax
import jax.numpy as jnp
from jax import lax
from jax.experimental import pallas as pl
from jax.experimental.pallas import tpu as pltpu
from jax.sharding import PartitionSpec as P

LAG_MAX = 2
ridge_weight = 0.05
COS_TERMS = (
    1.4142124652862549,
    -27.915136337280273,
    91.82308197021484,
    -120.5933837890625,
    83.14732360839844,
    -29.807071685791016,
)
ROUNDER = 12582912.0
INV_TWO_PI = 0.15915494309189535
CHUNK = 512
PIECES = 4
BLOCK = 8


def three_parts(x):
    hi = x.astype(jnp.bfloat16)
    rest = x - hi.astype(jnp.float32)
    mid = rest.astype(jnp.bfloat16)
    low = (rest - mid.astype(jnp.float32)).astype(jnp.bfloat16)
    return hi, mid, low


def turn_weights(freq_ref, phase_ref):
    r, k = freq_ref.shape
    rows = three_parts(freq_ref[...].astype(jnp.float32) * INV_TWO_PI)
    phase = three_parts(phase_ref[...] * INV_TWO_PI)
    rows = [part.astype(jnp.float32) for part in rows + phase]
    rest = jnp.zeros((r - len(phase), k), jnp.float32)
    return jnp.concatenate([*rows, rest], axis=0).T.astype(jnp.bfloat16)


def chunk_turns(weights, x):
    ones = jnp.ones(x.shape, jnp.bfloat16)
    return jnp.dot(
        weights, jnp.concatenate([x, x, x, ones], axis=0), preferred_element_type=jnp.float32
    )


def cosines(turns):
    part = turns - ((turns + ROUNDER) - ROUNDER)
    s = part * part
    total = jnp.full(s.shape, COS_TERMS[-1], jnp.float32)
    for term in COS_TERMS[-2::-1]:
        total = total * s + term
    return total.astype(jnp.bfloat16)


def features_kernel(weights_ref, factors_ref, features_ref):
    for i in range(factors_ref.shape[0]):
        for at in range(0, factors_ref.shape[2], CHUNK):
            span = pl.ds(at, CHUNK)
            features_ref[i, :, span] = cosines(
                chunk_turns(weights_ref[...], factors_ref[i, :, span])
            )


def packed(sums):
    k = sums.shape[1]
    half, quarter = k // 2, k // 4
    lane = lax.broadcasted_iota(jnp.int32, (quarter, k), 1)
    folded = jnp.where(lane < half, sums[:quarter], pltpu.roll(sums[quarter:half], half, 1))
    return jnp.concatenate([sums[k:], sums[half:k], folded], axis=0)


def unpacked(rows):
    k = rows.shape[1]
    half, quarter = k // 2, k // 4
    sets = rows.shape[0] - half - quarter
    low, folded = rows[sets : sets + half], rows[sets + half :]
    left = jnp.concatenate([folded, pltpu.roll(folded, half, 1)], axis=0)
    across = jnp.concatenate([left, low], axis=0).T[:half]
    lane = lax.broadcasted_iota(jnp.int32, (half, k), 1)
    return jnp.concatenate([jnp.where(lane < half, left, across), low], axis=0), rows[:sets]


def sums_kernel(first_ref, *refs):
    *given, factors_ref, flows_ref = refs[: -6 if len(refs) == 9 else -10]
    if len(given) == 1:
        features_ref, sums_ref, factors_here, flows_here, factor_sems, flow_sems = refs[-6:]
    else:
        features_ref, sums_ref, weights_out_ref, freq_here, phase_here = refs[-10:-5]
        factors_here, flows_here, factor_sems, flow_sems, weight_sems = refs[-5:]
        small = [
            pltpu.make_async_copy(source, here, weight_sems.at[i])
            for i, (source, here) in enumerate(zip(given, (freq_here, phase_here)))
        ]
        for copy in small:
            copy.start()
    dates, _, paths = features_ref.shape
    ats = [first_ref[0] + i for i in range(dates)]
    factor_loads = [
        pltpu.make_async_copy(factors_ref.at[t], factors_here.at[i], factor_sems.at[i])
        for i, t in enumerate(ats)
    ]
    flow_loads = [
        pltpu.make_async_copy(flows_ref.at[t], flows_here.at[i], flow_sems.at[i])
        for i, t in enumerate(ats)
    ]
    for pair in zip(factor_loads, flow_loads):
        for copy in pair:
            copy.start()
    if len(given) == 1:
        weights = given[0][...]
    else:
        for copy in small:
            copy.wait()
        weights = turn_weights(freq_here, phase_here)
        weights_out_ref[...] = weights
    items = [(i, pl.ds(at, CHUNK)) for i in range(dates) for at in range(0, paths, CHUNK)]
    arrived, joined = set(), set()

    def turns_of(item):
        i, span = item
        if i not in arrived:
            arrived.add(i)
            factor_loads[i].wait()
        return chunk_turns(weights, factors_here[i, :, span])

    def product_of(item, feats):
        i, span = item
        if i not in joined:
            joined.add(i)
            flow_loads[i].wait()
        both = jnp.concatenate([feats, flows_here[i, :, span]], axis=0)
        return lax.dot_general(
            both, feats, (((1,), (1,)), ((), ())), preferred_element_type=jnp.float32
        )

    turns, feats, sums = turns_of(items[0]), None, None
    for at in range(len(items) + 1):
        later = turns_of(items[at + 1]) if at + 1 < len(items) else None
        if at:
            i = items[at - 1][0]
            product = product_of(items[at - 1], feats)
            starts = at == 1 or items[at - 2][0] != i
            sums = product if starts else sums + product
            if at == len(items) or items[at][0] != i:
                sums_ref[i] = packed(sums)
        if at < len(items):
            i, span = items[at]
            feats = cosines(turns)
            features_ref[i, :, span] = feats
            turns = later


ON_CHIP = pl.BlockSpec(memory_space=pltpu.VMEM)
SCALARS = pl.BlockSpec(memory_space=pltpu.SMEM)
IN_HBM = pl.BlockSpec(memory_space=pltpu.HBM)


def in_hbm(a):
    return pltpu.with_memory_space_constraint(a, pltpu.HBM)


def params(mebibytes):
    return pltpu.CompilerParams(vmem_limit_bytes=mebibytes << 20)


def features_of(weights, factors):
    dates, r, paths = factors.shape
    k = weights.shape[0]
    return pl.pallas_call(
        features_kernel,
        in_specs=[ON_CHIP, ON_CHIP],
        out_specs=ON_CHIP,
        out_shape=jax.ShapeDtypeStruct((dates, k, paths), jnp.bfloat16),
        compiler_params=params(8),
        cost_estimate=pl.CostEstimate(
            flops=2000 * dates * k * paths, bytes_accessed=2 * dates * k * paths, transcendentals=0
        ),
        name="features",
    )(weights, factors)


def sums_of(first, dates, given, factors, flows):
    _, r, paths = factors.shape
    k, sets = given[0].shape[len(given) - 1], flows.shape[1]
    outs = [
        jax.ShapeDtypeStruct((dates, k, paths), jnp.bfloat16),
        jax.ShapeDtypeStruct((dates, sets + k // 2 + k // 4, k), jnp.float32),
    ]
    scratch = [
        pltpu.VMEM((dates, r, paths), jnp.bfloat16),
        pltpu.VMEM((dates, sets, paths), jnp.bfloat16),
        pltpu.SemaphoreType.DMA((dates,)),
        pltpu.SemaphoreType.DMA((dates,)),
    ]
    specs = [ON_CHIP]
    if len(given) == 2:
        outs.append(jax.ShapeDtypeStruct((k, 4 * r), jnp.bfloat16))
        scratch = [pltpu.VMEM(a.shape, a.dtype) for a in given] + scratch
        scratch.append(pltpu.SemaphoreType.DMA((2,)))
        specs = [IN_HBM, IN_HBM]
        given = map(in_hbm, given)
    return pl.pallas_call(
        sums_kernel,
        in_specs=[SCALARS, *specs, IN_HBM, IN_HBM],
        out_specs=(ON_CHIP,) * len(outs),
        out_shape=tuple(outs),
        scratch_shapes=scratch,
        compiler_params=params(14),
        cost_estimate=pl.CostEstimate(
            flops=20000 * dates * k * paths,
            bytes_accessed=4 * dates * k * paths,
            transcendentals=0,
        ),
        name="sums",
    )(first.reshape(1), *given, in_hbm(factors), in_hbm(flows))


def solve_kernel(paths_all, one_ref, two_ref, out_ref):
    k = one_ref.shape[1]
    system, right = unpacked((one_ref[...] + two_ref[...]) / paths_all)
    row_at = lax.broadcasted_iota(jnp.int32, (k, k), 0)
    lane_at = lax.broadcasted_iota(jnp.int32, (k, k), 1)
    system = system + jnp.where(row_at == lane_at, ridge_weight, 0.0)
    m = jnp.concatenate([system, right], axis=0)
    lane = lax.broadcasted_iota(jnp.int32, (1, k), 1)
    for j in range(0, k, BLOCK):
        pivots = [m[i : i + 1, :] for i in range(BLOCK)]
        entries = {
            (i, q): jnp.broadcast_to(pivots[i][:, j + q : j + q + 1], (1, k))
            for i in range(BLOCK)
            for q in range(i, BLOCK)
        }
        rows = [row - jnp.where(lane == j + i, 1.0, 0.0) for i, row in enumerate(pivots)]
        for p in range(BLOCK):
            inverse = 1.0 / entries[p, p]
            rows[p] = rows[p] * inverse
            scaled = {q: entries[p, q] * inverse for q in range(p + 1, BLOCK)}
            for i in range(BLOCK):
                if i != p:
                    factor = entries[min(i, p), max(i, p)]
                    rows[i] = rows[i] - factor * rows[p]
                    for q in range(max(i, p + 1), BLOCK):
                        entries[i, q] = entries[i, q] - factor * scaled[q]
            for q, entry in scaled.items():
                entries[p, q] = entry
        m = m[BLOCK:]
        m = m - sum(m[:, j + i : j + i + 1] * rows[i] for i in range(BLOCK))
    out_ref[...] = m.astype(jnp.bfloat16)


def solved(one, two, paths_all):
    k = one.shape[1]
    sets = one.shape[0] - k // 2 - k // 4
    return pl.pallas_call(
        functools.partial(solve_kernel, paths_all),
        in_specs=[ON_CHIP, ON_CHIP],
        out_specs=ON_CHIP,
        out_shape=jax.ShapeDtypeStruct((sets, k), jnp.bfloat16),
        compiler_params=params(8),
        name="solve",
    )(one, two)


def value_of(coefs, feats):
    return jnp.dot(coefs, feats, preferred_element_type=jnp.float32).astype(jnp.bfloat16)


def limits_of(lag_ref, threshold_ref, transfer_ref):
    def column(ref):
        return jnp.broadcast_to(ref[...], (128, ref.shape[1])).T

    offset = (column(threshold_ref) + column(transfer_ref)).astype(jnp.float32) / 100.0
    recent = jnp.where(column(lag_ref) == 1, 1.0, 0.0)
    times = CHUNK // 128
    return jnp.concatenate([offset] * times, axis=1), jnp.concatenate(
        [recent.astype(jnp.bfloat16)] * times, axis=1
    ) > 0.5


def exposed_of(v, last, before, offset, recent):
    lagged = jnp.where(recent, last, before).astype(jnp.float32)
    collateral = jnp.maximum(lagged - offset, 0.0)
    return jnp.maximum(v.astype(jnp.float32) - collateral, 0.0)


def by_lane(exposed):
    return sum(exposed[:, i : i + 128] for i in range(0, exposed.shape[1], 128))


def profile_of(totals, paths_all, dates):
    sets = next(iter(totals.values())).shape[0]
    lane = lax.broadcasted_iota(jnp.int32, (sets, 128), 1)
    sums = jnp.zeros((sets, 128), jnp.float32)
    for t, total in totals.items():
        here = jnp.sum(total, axis=1, keepdims=True) / paths_all
        sums = jnp.where(lane == t, here, sums)
    return sums.T[:dates]


def add_values(first_ref, coefs_ref, features_ref, values_ref):
    for i in range(features_ref.shape[0]):
        t = first_ref[0] + i
        for at in range(0, values_ref.shape[2], CHUNK):
            span = pl.ds(at, CHUNK)
            values_ref[t, :, span] = value_of(coefs_ref[i], features_ref[i, :, span])


def values_kernel(first_ref, coefs_ref, features_ref, *refs):
    add_values(first_ref, coefs_ref, features_ref, refs[-1])


def later_kernel(
    paths_all,
    first_ref,
    lag_ref,
    threshold_ref,
    transfer_ref,
    coefs_ref,
    features_ref,
    given_values_ref,
    exposure_ref,
    values_ref,
    profile_ref,
    staged_ref,
    sems,
):
    del given_values_ref
    add_values(first_ref, coefs_ref, features_ref, values_ref)
    dates, sets, paths = values_ref.shape
    offset, recent = limits_of(lag_ref, threshold_ref, transfer_ref)
    totals, copies = {}, []
    for t in range(LAG_MAX, dates):
        totals[t] = jnp.zeros((sets, 128), jnp.float32)
        for at in range(0, paths, CHUNK):
            span = pl.ds(at, CHUNK)
            exposed = exposed_of(
                *(values_ref[t - back, :, span] for back in range(LAG_MAX + 1)), offset, recent
            )
            staged_ref[t - LAG_MAX, :, span] = exposed.astype(jnp.bfloat16)
            totals[t] += by_lane(exposed)
            if (at + CHUNK) % (paths // PIECES) == 0:
                there = pl.ds(at + CHUNK - paths // PIECES, paths // PIECES)
                copies.append(
                    pltpu.make_async_copy(
                        staged_ref.at[t - LAG_MAX, :, there],
                        exposure_ref.at[t, :, there],
                        sems.at[len(copies)],
                    )
                )
                copies[-1].start()
    profile_ref[...] = profile_of(totals, paths_all, dates)
    for copy in copies:
        copy.wait()


def first_kernel(
    paths_all,
    lag_ref,
    threshold_ref,
    transfer_ref,
    prior_coefs_ref,
    prior_features_ref,
    values_ref,
    profile_in_ref,
    exposure_in_ref,
    exposure_ref,
    profile_ref,
    staged_ref,
    sems,
):
    del exposure_in_ref
    sets, paths = values_ref.shape[1:]
    offset, recent = limits_of(lag_ref, threshold_ref, transfer_ref)
    totals = {t: jnp.zeros((sets, 128), jnp.float32) for t in range(LAG_MAX)}
    copies, piece = [], paths // PIECES
    for at in range(0, paths, CHUNK):
        span = pl.ds(at, CHUNK)
        v = [value_of(prior_coefs_ref[i], prior_features_ref[i, :, span]) for i in range(LAG_MAX)]
        for t in range(LAG_MAX):
            v.append(values_ref[t, :, span])
            exposed = exposed_of(v[-1], v[-2], v[-3], offset, recent)
            staged_ref[t, :, span] = exposed.astype(jnp.bfloat16)
            totals[t] += by_lane(exposed)
        if (at + CHUNK) % piece == 0:
            there = pl.ds(at + CHUNK - piece, piece)
            copies.append(
                pltpu.make_async_copy(
                    staged_ref.at[:, :, there],
                    exposure_ref.at[pl.ds(0, LAG_MAX), :, there],
                    sems.at[len(copies)],
                )
            )
            copies[-1].start()
    profile = profile_in_ref[...] + profile_of(totals, paths_all, profile_in_ref.shape[0])
    flat = jnp.concatenate([profile[t : t + 1] for t in range(profile.shape[0])], axis=1)
    profile_ref[...] = jnp.broadcast_to(flat[None], profile_ref.shape)
    for copy in copies:
        copy.wait()


def values_of(first, coefs, features, dates, values=None):
    here, sets, k = coefs.shape
    paths = features.shape[2]
    given = () if values is None else (values,)
    return pl.pallas_call(
        values_kernel,
        in_specs=[SCALARS] + [ON_CHIP] * (2 + len(given)),
        out_specs=ON_CHIP,
        out_shape=jax.ShapeDtypeStruct((dates, sets, paths), jnp.bfloat16),
        input_output_aliases={3: 0} if given else {},
        compiler_params=params(4),
        cost_estimate=pl.CostEstimate(
            flops=200 * here * k * sets * paths,
            bytes_accessed=2 * here * (k + sets) * paths,
            transcendentals=0,
        ),
        name="values",
    )(first.reshape(1), coefs, features, *given)


def later_exposures(first, limits, coefs, features, values, paths_all):
    dates, sets, paths = values.shape
    args = (first.reshape(1), *limits, coefs, features, values)
    return pl.pallas_call(
        functools.partial(later_kernel, paths_all),
        in_specs=[SCALARS] + [ON_CHIP] * (len(args) - 1),
        out_specs=(IN_HBM, ON_CHIP, ON_CHIP),
        out_shape=(
            pltpu.HBM(values.shape, values.dtype),
            jax.ShapeDtypeStruct(values.shape, values.dtype),
            jax.ShapeDtypeStruct((dates, sets), jnp.float32),
        ),
        scratch_shapes=[
            pltpu.VMEM((dates - LAG_MAX, sets, paths), jnp.bfloat16),
            pltpu.SemaphoreType.DMA(((dates - LAG_MAX) * PIECES,)),
        ],
        input_output_aliases={len(args) - 1: 1},
        compiler_params=params(12),
        cost_estimate=pl.CostEstimate(
            flops=200 * dates * 128 * sets * paths,
            bytes_accessed=4 * dates * sets * paths,
            transcendentals=0,
        ),
        name="later",
    )(*args)


def first_exposures(limits, prior_coefs, prior_features, values, profile, exposure, paths_all):
    args = (*limits, prior_coefs, prior_features, values, profile, exposure)
    return pl.pallas_call(
        functools.partial(first_kernel, paths_all),
        in_specs=[ON_CHIP] * (len(args) - 1) + [IN_HBM],
        out_specs=(IN_HBM, ON_CHIP),
        out_shape=(
            pltpu.HBM(exposure.shape, exposure.dtype),
            jax.ShapeDtypeStruct((lax.axis_size("path"), 1, profile.size), profile.dtype),
        ),
        scratch_shapes=[
            pltpu.VMEM((LAG_MAX, *values.shape[1:]), jnp.bfloat16),
            pltpu.SemaphoreType.DMA((PIECES,)),
        ],
        input_output_aliases={len(args) - 1: 0},
        compiler_params=params(8),
        name="first",
    )(*args)


def total_kernel(parts_ref, total_ref):
    flat = jnp.sum(parts_ref[...], axis=0)
    dates, sets = total_ref.shape
    for t in range(dates):
        total_ref[t : t + 1, :] = flat[:, t * sets : (t + 1) * sets]


def total_of(parts, shape):
    return pl.pallas_call(
        total_kernel,
        in_specs=[ON_CHIP],
        out_specs=ON_CHIP,
        out_shape=jax.ShapeDtypeStruct(shape, parts.dtype),
        name="total",
    )(pltpu.with_memory_space_constraint(parts, pltpu.VMEM))


CORE, ROW, NEAR, NEXT, FAR = 1, 2, 4, 8, 24


def swapped(value, step):
    return lax.ppermute(value, "path", [(i, i ^ step) for i in range(lax.axis_size("path"))])


def picked(value, low):
    return jnp.where(low, value[0], value[1])


def ordered(mine, other, low):
    first = jnp.where(low, mine, other)
    second = jnp.where(low, other, mine)
    return jnp.concatenate([first, second], axis=0)


def from_earlier(value):
    length = lax.axis_size("date")
    return lax.ppermute(value, "date", [(i, i + 1) for i in range(length - 1)])


def local(factors, cashflows, frequency, phases, margin_lag, thresholds, transfer_min):
    paths_all = factors.shape[2] * lax.axis_size("path")
    me = lax.axis_index("path").astype(jnp.uint32)
    core, row, near = (((me >> bit) & 1).astype(jnp.int32) for bit in range(3))
    half = factors.shape[0] // 2
    quarter = half // 2
    firsts = (half * (1 - core), half * core + quarter * (1 - row), half * core + quarter * row)
    first_a, first_b, first_c, core_low, row_low, near_low = lax.optimization_barrier(
        (*firsts, core == 0, row == 0, near == 0)
    )
    prior_factors = from_earlier(factors[-LAG_MAX:])
    given = (frequency.T, phases.reshape(1, -1))
    part_a, sums_a, weights = sums_of(first_a, half, given, factors, cashflows)
    from_core = swapped(sums_a, CORE).reshape(2, quarter, *sums_a.shape[1:])
    first_b, prior_factors = lax.optimization_barrier((first_b, prior_factors))
    part_b, sums_b = sums_of(first_b, quarter, (weights,), factors, cashflows)
    from_row = swapped(sums_b + picked(from_core[::-1], row_low), ROW)
    part_c, sums_c = sums_of(first_c, quarter, (weights,), factors, cashflows)
    kept = sums_c + picked(from_core, row_low) + from_row
    kept = picked(kept, near_low) + swapped(picked(kept[::-1], near_low), NEAR)
    kept = kept + swapped(kept, NEXT)
    prior_features = features_of(weights, prior_factors)
    from_far, prior_features = lax.optimization_barrier((swapped(kept, FAR), prior_features))
    coefs = solved(kept, from_far, paths_all)
    dates = factors.shape[0]
    coefs_c = ordered(coefs[None], swapped(coefs[None], NEAR), near_low)
    coefs_b = swapped(coefs_c, ROW)
    values = values_of(first_c, coefs_c, part_c, dates)
    coefs_here = ordered(coefs_c, coefs_b, row_low)
    coefs_a = swapped(coefs_here, CORE)
    values = values_of(first_b, coefs_b, part_b, dates, values)
    last_coefs = jnp.where(core_low, coefs_a[-LAG_MAX:], coefs_here[-LAG_MAX:])
    prior_coefs = from_earlier(last_coefs)
    limits = tuple(a.reshape(1, -1) for a in (margin_lag, thresholds, transfer_min))
    exposure, values, profile = later_exposures(
        first_a, limits, coefs_a, part_a, values, paths_all
    )
    exposure, parts = first_exposures(
        limits, prior_coefs, prior_features, values, profile, exposure, paths_all
    )
    return exposure, total_of(lax.all_to_all(parts, "path", 0, 0, tiled=True), profile.shape)


def solution(mesh):
    return jax.shard_map(
        local,
        mesh=mesh,
        in_specs=(P("date", None, "path"), P("date", None, "path"), P(), P(), P(), P(), P()),
        out_specs=(P("date", None, "path"), P("date", None)),
        check_vma=False,
    )
```
